256 devices in a mesh: bank: 128 (over y, z, x), sub: 2 (over core).
Axes of the slice: x: 4, y: 4, z: 8, core: 2. Of those that a mesh axis runs over, the one named last changes fastest.
Arguments:
- embeddings: bfloat16 [786432, 1024], P(('bank', 'sub'))
- pivots: int32 [2, 256], replicated, may hold values from 0 to 786431, as said below
Outputs:
- basis: float32 [786432, 512], P(('bank', 'sub'))
- triangle: float32 [512, 512], replicated
The draws below stay inside these ranges and needn't reach their ends.
Inputs may be any that keep to these rules, and one draw needn't show every extreme that they name: All 512 entries are distinct molecules. Molecule g lies on device g // 3072 of bank+sub (bank slowest). Each device holds at most 1 pivots of each block step, and some device holds exactly 1.
All inputs are finite; a program needn't handle non-finite values.
Results may differ from the reference program's by a relative error of at most 0.0003.
Values may be sent and summed in bfloat16 or wider, within the bound.
A program may use at most 64 MiB of HBM per device.

```python
import jax
import jax.numpy as jnp
from jax import lax

D = 1024
P_SIZE = 256
R_DEV = 3072
NROWS = 786432
N_BANK = 128
N_SUB = 2


def draw_embeddings(key, part):
    key_base = jax.random.fold_in(key, 11)
    key_amp = jax.random.fold_in(key, 12)
    key_noise = jax.random.fold_in(key, 13)
    direction = jax.random.normal(key_base, (D,), jnp.float32)
    amplitude = jax.random.uniform(key_amp, (NROWS, 1), jnp.float32, 0.2, 0.8)
    noise = jax.random.normal(key_noise, (NROWS, D), jnp.float32)
    values = amplitude * direction[None, :] + noise
    return values.astype(jnp.bfloat16)


def draw_pivots(key, part):
    device_count = N_BANK * N_SUB
    capacity = (P_SIZE + device_count - 1) // device_count
    band = R_DEV // (2 * capacity)
    lists = []
    for which in range(2):
        base_key = jax.random.fold_in(key, 100 + which)
        order = jax.random.permutation(jax.random.fold_in(base_key, 1), P_SIZE).astype(jnp.int32)
        mapping = jax.random.permutation(jax.random.fold_in(base_key, 2), device_count).astype(jnp.int32)
        offsets = jax.random.randint(jax.random.fold_in(base_key, 3), (P_SIZE,), 0, band, jnp.int32)
        owners = mapping[order % device_count]
        ranking = order // device_count
        local_rows = which * (R_DEV // 2) + ranking * band + offsets
        lists.append(owners * R_DEV + local_rows)
    return jnp.stack(lists, axis=0).astype(jnp.int32)


def setup_inputs(seed: int = 0) -> dict:
    seeds = jax.random.split(jax.random.key(seed), 3)
    embeddings = draw_embeddings(jax.random.fold_in(seeds[2], 71), 0)
    pivots = draw_pivots(jax.random.fold_in(seeds[2], 71), 0)
    return dict(embeddings=embeddings, pivots=pivots)


def lower_inverse(factor):
    identity = jnp.eye(factor.shape[0], dtype=factor.dtype)
    return lax.linalg.triangular_solve(factor, identity, left_side=True, lower=True)

def reference(embeddings, pivots):
    highest = lax.Precision.HIGHEST
    flat_list = pivots.reshape(-1).astype(jnp.int32)
    widened = embeddings.astype(jnp.float32)
    norms = jnp.sum(widened * widened, axis=1)
    chosen = embeddings[flat_list]
    chosen_norms = norms[flat_list]
    dots = jnp.dot(embeddings.astype(jnp.float32), chosen.T.astype(jnp.float32), preferred_element_type=jnp.float32)
    similar = dots / (norms[:, None] + chosen_norms[None, :] - dots)
    block_dots = jnp.dot(chosen.astype(jnp.float32), chosen.T.astype(jnp.float32), preferred_element_type=jnp.float32)
    block = block_dots / (chosen_norms[:, None] + chosen_norms[None, :] - block_dots)
    first_inverse = lower_inverse(jnp.linalg.cholesky(block[:P_SIZE, :P_SIZE]))
    first_factor = jnp.dot(similar[:, :P_SIZE], first_inverse.T, precision=highest)
    pivot_first = jnp.dot(block[P_SIZE:, :P_SIZE], first_inverse.T, precision=highest)
    second_cols = similar[:, P_SIZE:] - jnp.dot(first_factor, pivot_first.T, precision=highest)
    second_block = block[P_SIZE:, P_SIZE:] - jnp.dot(pivot_first, pivot_first.T, precision=highest)
    second_inverse = lower_inverse(jnp.linalg.cholesky(second_block))
    second_factor = jnp.dot(second_cols, second_inverse.T, precision=highest)
    factor = jnp.concatenate([first_factor, second_factor], axis=1)
    gram = jnp.dot(factor.T, factor, precision=highest) / factor.shape[0]
    lower_root = jnp.linalg.cholesky(gram)
    basis = jnp.dot(factor, lower_inverse(lower_root).T, precision=highest)
    return (basis, lower_root.T)
```

```python
import jax
import jax.numpy as jnp
from jax import lax
from jax.experimental import pallas as pl
from jax.experimental.pallas import tpu as pltpu
from jax.sharding import PartitionSpec as P

HI = lax.Precision.HIGHEST
F32 = jnp.float32
BF16 = jnp.bfloat16
P_SIZE = 256
NX, NY, NZ = 4, 4, 8
NB = 64
TILE = 512
UPPER = [(i, j) for i in range(4) for j in range(i, 4)]
MESH = pl.DeviceIdType.MESH


def dot(a, b, dims, precision=None):
    return lax.dot_general(a, b, ((dims[:1], dims[1:]), ((), ())), precision=precision, preferred_element_type=F32)


def base_block(rows):
    count = NB // 8
    rows = list(rows)
    sub = lax.broadcasted_iota(jnp.int32, (8, 128), 0)
    full = lambda v: jnp.broadcast_to(v, (8, 128))
    out = []
    for k in range(count):
        cols = [[full(rows[t][:, 8 * k + c : 8 * k + c + 1]) for c in range(8)] for t in range(k, count)]
        scale = jnp.zeros((8, 128), F32)
        for c in range(8):
            pivot = full(cols[0][c][c : c + 1, :])
            pivot_row = full(rows[k][c : c + 1, :])
            ahead = [full(cols[0][e][c : c + 1, :]) for e in range(c + 1, 8)]
            inverse = 1.0 / pivot
            scale = jnp.where(sub == c, pivot, scale)
            for t in range(k, count):
                mult = cols[t - k][c] * inverse
                if t == k:
                    mult = jnp.where(sub > c, mult, 0.0)
                rows[t] = rows[t] - mult * pivot_row
                for e in range(c + 1, 8):
                    cols[t - k][e] = cols[t - k][e] - mult * ahead[e - c - 1]
        out.append(rows[k] * lax.rsqrt(scale))
    return out


def cholesky_inverse(w_ref, diag_ref):
    n = w_ref.shape[0]
    lane = lax.broadcasted_iota(jnp.int32, (8, 128), 1)
    sub = lax.broadcasted_iota(jnp.int32, (8, 128), 0)
    for k in range(n // NB):
        r0 = k * NB
        left = (r0 // 128) * 128
        rows = []
        for t in range(NB // 8):
            block = w_ref[r0 + 8 * t : r0 + 8 * t + 8, left : left + 128]
            if r0 % 128:
                block = pltpu.roll(block, 64, 1)
            rows.append(jnp.where(lane < 64, block, jnp.where(lane - 64 == sub + 8 * t, 1.0, 0.0)))
        both = jnp.concatenate(base_block(rows), axis=0)
        diag_ref[k] = both
        wide = w_ref[r0 : r0 + NB, :]
        col = lax.broadcasted_iota(jnp.int32, (NB, n), 1)
        row = lax.broadcasted_iota(jnp.int32, (NB, n), 0)
        wide = jnp.where((col >= r0) & (col < r0 + NB), jnp.where(col - r0 == row, 1.0, 0.0), wide)
        strip = dot(both[:, 64:], wide, (1, 0), HI)
        w_ref[r0 : r0 + NB, :] = strip
        if r0 + NB < n:
            rest = n - r0 - NB
            update = dot(strip[:, r0 + NB :], strip, (0, 0), HI)
            current = w_ref[r0 + NB :, :]
            col = lax.broadcasted_iota(jnp.int32, (rest, n), 1)
            current = jnp.where((col >= r0) & (col < r0 + NB), 0.0, current)
            w_ref[r0 + NB :, :] = current - update


def lower_blocks(w):
    n = w.shape[0]
    row = lax.broadcasted_iota(jnp.int32, (n, n), 0)
    col = lax.broadcasted_iota(jnp.int32, (n, n), 1)
    return jnp.where(row >= col, w, 0.0)


def coords():
    bank = lax.axis_index("bank")
    core = lax.axis_index("sub")
    x = lax.rem(bank, NX)
    z = lax.rem(bank // NX, NZ)
    y = bank // (NX * NZ)
    return x, y, z, core


def bank_of(x, y, z):
    return (y * NZ + z) * NX + x


def greet(peers):
    barrier = pltpu.get_barrier_semaphore()
    for peer in peers:
        pl.semaphore_signal(barrier, inc=1, device_id=peer, device_id_type=MESH)
    pl.semaphore_wait(barrier, len(peers))


def axis_peers(x, y, z, core):
    along_x = [(bank_of(lax.rem(x + o, NX), y, z), core) for o in range(1, NX)]
    along_y = [(bank_of(x, lax.rem(y + o, NY), z), core) for o in range(1, NY)]
    along_z = [(bank_of(x, y, lax.rem(z + o, NZ)), core) for o in range(1, NZ)]
    return along_x, along_y, along_z


def gather_kernel(mine_ref, out_ref, send, recv):
    x, y, z, core = coords()
    other = (lax.axis_index("bank"), 1 - core)
    along_x, along_y, along_z = axis_peers(x, y, z, core)
    half = NX * NY * NZ
    slot_a = core * half + (y * NZ + z) * NX + x
    slot_b = core * half + (x * NZ + z) * NY + y
    local = pltpu.make_async_copy(mine_ref.at[0], out_ref.at[0, slot_a], send.at[0])
    local_b = pltpu.make_async_copy(mine_ref.at[1], out_ref.at[1, slot_b], send.at[1])
    local.start()
    local_b.start()
    greet([other] + along_x + along_y + along_z)
    local.wait()
    local_b.wait()
    count = [2]

    def push(step, start, size, peers):
        copies = []
        for peer in peers:
            i = count[0]
            count[0] += 1
            part = out_ref.at[step, pl.ds(start, size)]
            copy = pltpu.make_async_remote_copy(
                src_ref=part, dst_ref=part, send_sem=send.at[i], recv_sem=recv.at[i], device_id=peer, device_id_type=MESH
            )
            copy.start()
            copies.append(copy)
        return copies

    base = core * half
    first_a = push(0, base + (y * NZ + z) * NX + x, 1, along_x)
    first_b = push(1, base + (x * NZ + z) * NY + y, 1, along_y)
    for copy in first_a:
        copy.wait_recv()
    second_a = push(0, base + (y * NZ + z) * NX, NX, along_z)
    for copy in first_b:
        copy.wait_recv()
    second_b = push(1, base + (x * NZ + z) * NY, NY, along_z)
    for copy in second_a:
        copy.wait_recv()
    third_a = push(0, base + y * NZ * NX, NZ * NX, along_y)
    for copy in second_b:
        copy.wait_recv()
    third_b = push(1, base + x * NZ * NY, NZ * NY, along_x)
    for copy in third_a:
        copy.wait_recv()
    last_a = push(0, base, half, [other])
    for copy in third_b:
        copy.wait_recv()
    last_b = push(1, base, half, [other])
    for copy in last_a + last_b:
        copy.wait_recv()
    for copy in first_a + first_b + second_a + second_b + third_a + third_b + last_a + last_b:
        copy.wait_send()


def gather_rows(mine):
    copies = 2 + 2 * (3 + 7 + 3 + 1)
    return pl.pallas_call(
        gather_kernel,
        out_shape=jax.ShapeDtypeStruct((2, 256, 8, 128), BF16),
        in_specs=[pl.BlockSpec(memory_space=pltpu.VMEM)],
        out_specs=pl.BlockSpec(memory_space=pltpu.VMEM),
        scratch_shapes=[pltpu.SemaphoreType.DMA((copies,)), pltpu.SemaphoreType.DMA((copies,))],
        compiler_params=pltpu.CompilerParams(collective_id=0, has_side_effects=True),
        name="gather_rows",
    )(mine)


def factor_kernel(targets_ref, rows_ref, emb_ref, factor_ref, gram_ref, wide_ref, chosen_ref, w_ref, inv_ref, diag_ref, norm_ref):
    step = pl.program_id(0)

    @pl.when(step == 0)
    def _():
        for s in range(2):
            slot = lax.broadcasted_iota(jnp.int32, (256, 256), 0)
            pick = jnp.where(slot == targets_ref[s : s + 1, :], 1.0, 0.0).astype(BF16)
            wide_ref[...] = rows_ref[s].reshape(2048, 128).astype(F32)
            for q in range(8):
                part = wide_ref[pl.ds(q, 256, stride=8), :].astype(BF16)
                chosen_ref[256 * s : 256 * s + 256, 128 * q : 128 * q + 128] = dot(pick, part, (0, 0)).astype(BF16)
        dots = dot(chosen_ref[...], chosen_ref[...], (1, 1))
        row = lax.broadcasted_iota(jnp.int32, (512, 512), 0)
        col = lax.broadcasted_iota(jnp.int32, (512, 512), 1)
        own = jnp.where(row == col, dots, 0.0)
        norm_row = jnp.sum(own, axis=0, keepdims=True)
        norm_ref[...] = norm_row
        w_ref[...] = dots / (jnp.sum(own, axis=1, keepdims=True) + norm_row - dots)
        cholesky_inverse(w_ref, diag_ref)
        inv_ref[...] = lower_blocks(w_ref[...])
        gram_ref[...] = jnp.zeros_like(gram_ref)

    emb = emb_ref[...]
    wide = emb.astype(F32)
    norms = jnp.sum(wide * wide, axis=1, keepdims=True)
    dots = dot(emb, chosen_ref[...], (1, 1))
    similar = dots / (norms + norm_ref[...] - dots)
    factor = dot(similar, inv_ref[...], (1, 1), HI)
    factor_ref[...] = factor
    for b, (i, j) in enumerate(UPPER):
        if i == j:
            part = dot(factor[:, 128 * i : 128 * i + 128], factor[:, 128 * i :], (0, 0), HI)
            for e in range(4 - i):
                gram_ref[b + e] += part[:, 128 * e : 128 * e + 128]


def factor_call(targets, rows, embeddings):
    count = embeddings.shape[0] // TILE
    vmem = lambda shape: pl.BlockSpec(shape, lambda i: (0,) * len(shape))
    return pl.pallas_call(
        factor_kernel,
        grid=(count,),
        out_shape=(
            jax.ShapeDtypeStruct((embeddings.shape[0], 512), F32),
            jax.ShapeDtypeStruct((10, 128, 128), F32),
        ),
        in_specs=[vmem((2, 256)), vmem((2, 256, 8, 128)), pl.BlockSpec((TILE, 1024), lambda i: (i, 0))],
        out_specs=(pl.BlockSpec((TILE, 512), lambda i: (i, 0)), vmem((10, 128, 128))),
        scratch_shapes=[
            pltpu.VMEM((2048, 128), F32),
            pltpu.VMEM((512, 1024), BF16),
            pltpu.VMEM((512, 512), F32),
            pltpu.VMEM((512, 512), F32),
            pltpu.VMEM((8, NB, 128), F32),
            pltpu.VMEM((1, 512), F32),
        ],
        compiler_params=pltpu.CompilerParams(vmem_limit_bytes=56 << 20, dimension_semantics=("arbitrary",)),
        name="factor",
    )(targets, rows, embeddings)


STREAMS = ((0, 384), (384, 256))


def reduce_kernel(in_ref, out_ref, core_in, big_in, small_in, z_in, half_sum, big_sum, small_sum, send, recv):
    x, y, z, core = coords()
    other = (lax.axis_index("bank"), 1 - core)
    along_x, along_y, along_z = axis_peers(x, y, z, core)
    greet([other] + along_x + along_y + along_z)
    count = [0]
    everything = []

    def push(src, dst, peer):
        i = count[0]
        count[0] += 1
        copy = pltpu.make_async_remote_copy(
            src_ref=src, dst_ref=dst, send_sem=send.at[i], recv_sem=recv.at[i], device_id=peer, device_id_type=MESH
        )
        copy.start()
        everything.append(copy)
        return copy

    mine = core * 640
    theirs = (1 - core) * 640
    axes = ((along_x, NX, x), (along_y, NY, y))
    state = []
    for s, (start, size) in enumerate(STREAMS):
        state.append(push(in_ref.at[pl.ds(theirs + start, size)], core_in.at[pl.ds(start, size)], other))
    big = []
    for s, (start, size) in enumerate(STREAMS):
        peers, n, pos = axes[s]
        state[s].wait_recv()
        half_sum[pl.ds(start, size), :] = in_ref[pl.ds(mine + start, size), :] + core_in[pl.ds(start, size), :]
        part = size // 4
        copies = []
        for o in range(1, n):
            to = lax.rem(pos + o, n)
            copies.append(
                push(
                    half_sum.at[pl.ds(start + to * part, part)],
                    big_in.at[o - 1, pl.ds(start // 4, part)],
                    peers[o - 1],
                )
            )
        big.append(copies)
    small = []
    for s, (start, size) in enumerate(STREAMS):
        _, n, pos = axes[s]
        peers, n2, pos2 = axes[1 - s]
        part = size // 4
        for copy in big[s]:
            copy.wait_recv()
        total = half_sum[pl.ds(start + pos * part, part), :]
        for o in range(n - 1):
            total = total + big_in[o, start // 4 : start // 4 + part, :]
        big_sum[start // 4 : start // 4 + part, :] = total
        tiny = part // 4
        copies = []
        for o in range(1, n2):
            to = lax.rem(pos2 + o, n2)
            copies.append(
                push(
                    big_sum.at[pl.ds(start // 4 + to * tiny, tiny)],
                    small_in.at[o - 1, pl.ds(start // 16, tiny)],
                    peers[o - 1],
                )
            )
        small.append(copies)
    last = []
    for s, (start, size) in enumerate(STREAMS):
        _, n2, pos2 = axes[1 - s]
        tiny = size // 16
        for copy in small[s]:
            copy.wait_recv()
        total = big_sum[pl.ds(start // 4 + pos2 * tiny, tiny), :]
        for o in range(n2 - 1):
            total = total + small_in[o, start // 16 : start // 16 + tiny, :]
        small_sum[start // 16 : start // 16 + tiny, :] = total
        piece = small_sum.at[pl.ds(start // 16, tiny)]
        last.append([push(piece, z_in.at[z, pl.ds(start // 16, tiny)], peer) for peer in along_z])
        z_in[z, start // 16 : start // 16 + tiny, :] = total
    back = []
    for s, (start, size) in enumerate(STREAMS):
        _, n, pos = axes[s]
        peers, n2, pos2 = axes[1 - s]
        part, tiny = size // 4, size // 16
        for copy in last[s]:
            copy.wait_recv()
        total = z_in[0, start // 16 : start // 16 + tiny, :]
        for o in range(1, NZ):
            total = total + z_in[o, start // 16 : start // 16 + tiny, :]
        at = mine + start + pos * part + pos2 * tiny
        out_ref[pl.ds(at, tiny), :] = total
        piece = out_ref.at[pl.ds(at, tiny)]
        back.append([push(piece, piece, peer) for peer in peers])
    far = []
    for s, (start, size) in enumerate(STREAMS):
        peers, n, pos = axes[s]
        part = size // 4
        for copy in back[s]:
            copy.wait_recv()
        piece = out_ref.at[pl.ds(mine + start + pos * part, part)]
        far.append([push(piece, piece, peer) for peer in peers])
    final = []
    for s, (start, size) in enumerate(STREAMS):
        for copy in far[s]:
            copy.wait_recv()
        piece = out_ref.at[pl.ds(mine + start, size)]
        final.append(push(piece, piece, other))
    for copy in final:
        copy.wait_recv()
    for copy in everything:
        copy.wait_send()


def reduce_gram(gram):
    copies = 2 * (1 + 3 + 3 + 7 + 3 + 3 + 1)
    return pl.pallas_call(
        reduce_kernel,
        out_shape=jax.ShapeDtypeStruct((1280, 128), F32),
        in_specs=[pl.BlockSpec(memory_space=pltpu.VMEM)],
        out_specs=pl.BlockSpec(memory_space=pltpu.VMEM),
        scratch_shapes=[
            pltpu.VMEM((640, 128), F32),
            pltpu.VMEM((3, 160, 128), F32),
            pltpu.VMEM((3, 40, 128), F32),
            pltpu.VMEM((NZ, 40, 128), F32),
            pltpu.VMEM((640, 128), F32),
            pltpu.VMEM((160, 128), F32),
            pltpu.VMEM((40, 128), F32),
            pltpu.SemaphoreType.DMA((copies,)),
            pltpu.SemaphoreType.DMA((copies,)),
        ],
        compiler_params=pltpu.CompilerParams(collective_id=1, has_side_effects=True),
        name="reduce_gram",
    )(gram.reshape(1280, 128)).reshape(10, 128, 128)


def basis_kernel(total_rows, gram_ref, factor_ref, basis_ref, triangle_ref, w_ref, inv_ref, diag_ref):
    @pl.when(pl.program_id(0) == 0)
    def _():
        for b, (i, j) in enumerate(UPPER):
            w_ref[128 * i : 128 * i + 128, 128 * j : 128 * j + 128] = gram_ref[b] / total_rows
        cholesky_inverse(w_ref, diag_ref)
        w = w_ref[...]
        inv_ref[...] = lower_blocks(w)
        row = lax.broadcasted_iota(jnp.int32, (512, 512), 0)
        col = lax.broadcasted_iota(jnp.int32, (512, 512), 1)
        triangle_ref[...] = jnp.where(row < col, w, 0.0)
        low = lax.broadcasted_iota(jnp.int32, (NB, 128), 1)
        sub = lax.broadcasted_iota(jnp.int32, (NB, 128), 0)
        for k in range(8):
            left = 128 * (k // 2)
            both = diag_ref[k]
            keep = triangle_ref[NB * k : NB * k + NB, left : left + 128]
            if k % 2:
                mine = pltpu.roll(both, 64, 1)
                keep = jnp.where(low >= 64, jnp.where(low - 64 >= sub, mine, 0.0), keep)
            else:
                keep = jnp.where(low < 64, jnp.where(low >= sub, both, 0.0), keep)
            triangle_ref[NB * k : NB * k + NB, left : left + 128] = keep

    factor = factor_ref[...]
    inverse = inv_ref[...]
    basis_ref[:, :256] = dot(factor[:, :256], inverse[:256, :256], (1, 1), HI)
    basis_ref[:, 256:] = dot(factor, inverse[256:, :], (1, 1), HI)


def basis_call(gram, factor, total_rows):
    import functools

    count = factor.shape[0] // TILE
    vmem = lambda shape: pl.BlockSpec(shape, lambda i: (0,) * len(shape))
    return pl.pallas_call(
        functools.partial(basis_kernel, total_rows),
        grid=(count,),
        out_shape=(jax.ShapeDtypeStruct(factor.shape, F32), jax.ShapeDtypeStruct((512, 512), F32)),
        in_specs=[vmem((10, 128, 128)), pl.BlockSpec((TILE, 512), lambda i: (i, 0))],
        out_specs=(pl.BlockSpec((TILE, 512), lambda i: (i, 0)), vmem((512, 512))),
        scratch_shapes=[pltpu.VMEM((512, 512), F32), pltpu.VMEM((512, 512), F32), pltpu.VMEM((8, NB, 128), F32)],
        compiler_params=pltpu.CompilerParams(vmem_limit_bytes=56 << 20, dimension_semantics=("arbitrary",)),
        name="basis",
    )(gram, factor)


def per_device(embeddings, pivots):
    row_count = embeddings.shape[0]
    device_count = lax.axis_size(("bank", "sub"))
    me = lax.axis_index(("bank", "sub"))
    owner = pivots // row_count
    local = jnp.sum(jnp.where(owner == me, pivots - me * row_count, 0), axis=1)
    mine = jnp.stack([lax.dynamic_slice(embeddings, (local[s], 0), (1, 1024)).reshape(8, 128) for s in range(2)])
    bank, core = owner // 2, owner % 2
    bx, bz, by = bank % NX, (bank // NX) % NZ, bank // (NX * NZ)
    targets = jnp.stack([(core * 128 + bank)[0], (core * 128 + (bx * NZ + bz) * NY + by)[1]])
    rows = gather_rows(mine)
    factor, gram = factor_call(targets, rows, embeddings)
    gram = reduce_gram(gram)
    return basis_call(gram, factor, float(row_count * device_count))


def solution(mesh):
    in_specs = (P(("bank", "sub"), None), P())
    out_specs = (P(("bank", "sub"), None), P())
    return jax.shard_map(per_device, mesh=mesh, in_specs=in_specs, out_specs=out_specs, check_vma=False)
```

```python
import functools

import jax
import jax.numpy as jnp
from jax import lax
from jax.experimental import pallas as pl
from jax.experimental.pallas import tpu as pltpu
from jax.sharding import PartitionSpec as P

HI = lax.Precision.HIGHEST
F32 = jnp.float32
BF16 = jnp.bfloat16
P_SIZE = 256
NX, NY, NZ = 4, 4, 8
NB = 64
TILE = 512
UPPER = [(i, j) for i in range(4) for j in range(i, 4)]
MESH = pl.DeviceIdType.MESH


def dot(a, b, dims, precision=None):
    return lax.dot_general(a, b, ((dims[:1], dims[1:]), ((), ())), precision=precision, preferred_element_type=F32)


def base_block(rows):
    count = NB // 8
    rows = list(rows)
    sub = lax.broadcasted_iota(jnp.int32, (8, 128), 0)
    full = lambda v: jnp.broadcast_to(v, (8, 128))
    out = []
    for k in range(count):
        cols = [[full(rows[t][:, 8 * k + c : 8 * k + c + 1]) for c in range(8)] for t in range(k, count)]
        scale = jnp.zeros((8, 128), F32)
        for c in range(8):
            pivot = full(cols[0][c][c : c + 1, :])
            pivot_row = full(rows[k][c : c + 1, :])
            ahead = [full(cols[0][e][c : c + 1, :]) for e in range(c + 1, 8)]
            inverse = 1.0 / pivot
            scale = jnp.where(sub == c, pivot, scale)
            for t in range(k, count):
                mult = cols[t - k][c] * inverse
                if t == k:
                    mult = jnp.where(sub > c, mult, 0.0)
                rows[t] = rows[t] - mult * pivot_row
                for e in range(c + 1, 8):
                    cols[t - k][e] = cols[t - k][e] - mult * ahead[e - c - 1]
        out.append(rows[k] * lax.rsqrt(scale))
    return out


def cholesky_steps(w_ref, diag_ref):
    n = w_ref.shape[0]
    lane = lax.broadcasted_iota(jnp.int32, (8, 128), 1)
    sub = lax.broadcasted_iota(jnp.int32, (8, 128), 0)
    for k in range(n // NB):
        r0 = k * NB
        left = (r0 // 128) * 128
        rows = []
        for t in range(NB // 8):
            block = w_ref[r0 + 8 * t : r0 + 8 * t + 8, left : left + 128]
            if r0 % 128:
                block = pltpu.roll(block, 64, 1)
            rows.append(jnp.where(lane < 64, block, jnp.where(lane - 64 == sub + 8 * t, 1.0, 0.0)))
        both = jnp.concatenate(base_block(rows), axis=0)
        diag_ref[k] = both
        yield
        wide = w_ref[r0 : r0 + NB, :]
        col = lax.broadcasted_iota(jnp.int32, (NB, n), 1)
        row = lax.broadcasted_iota(jnp.int32, (NB, n), 0)
        wide = jnp.where((col >= r0) & (col < r0 + NB), jnp.where(col - r0 == row, 1.0, 0.0), wide)
        strip = dot(both[:, 64:], wide, (1, 0), HI)
        w_ref[r0 : r0 + NB, :] = strip
        if r0 + NB < n:
            rest = n - r0 - NB
            update = dot(strip[:, r0 + NB :], strip, (0, 0), HI)
            current = w_ref[r0 + NB :, :]
            col = lax.broadcasted_iota(jnp.int32, (rest, n), 1)
            current = jnp.where((col >= r0) & (col < r0 + NB), 0.0, current)
            w_ref[r0 + NB :, :] = current - update
        yield


def cholesky_inverse(w_ref, diag_ref):
    for _ in cholesky_steps(w_ref, diag_ref):
        pass


def lower_blocks(w):
    n = w.shape[0]
    row = lax.broadcasted_iota(jnp.int32, (n, n), 0)
    col = lax.broadcasted_iota(jnp.int32, (n, n), 1)
    return jnp.where(row >= col, w, 0.0)


def coords():
    bank = lax.axis_index("bank")
    core = lax.axis_index("sub")
    x = lax.rem(bank, NX)
    z = lax.rem(bank // NX, NZ)
    y = bank // (NX * NZ)
    return x, y, z, core


def bank_of(x, y, z):
    return (y * NZ + z) * NX + x


def greet(peers):
    barrier = pltpu.get_barrier_semaphore()
    for peer in peers:
        pl.semaphore_signal(barrier, inc=1, device_id=peer, device_id_type=MESH)
    pl.semaphore_wait(barrier, len(peers))


def axis_peers(x, y, z, core):
    along_x = [(bank_of(lax.rem(x + o, NX), y, z), core) for o in range(1, NX)]
    along_y = [(bank_of(x, lax.rem(y + o, NY), z), core) for o in range(1, NY)]
    along_z = [(bank_of(x, y, lax.rem(z + o, NZ)), core) for o in range(1, NZ)]
    return along_x, along_y, along_z


def gather_kernel(mine_ref, out_ref, send, recv):
    x, y, z, core = coords()
    other = (lax.axis_index("bank"), 1 - core)
    along_x, along_y, along_z = axis_peers(x, y, z, core)
    half = NX * NY * NZ
    slot_a = core * half + (y * NZ + z) * NX + x
    slot_b = core * half + (x * NZ + z) * NY + y
    local = pltpu.make_async_copy(mine_ref.at[0], out_ref.at[0, slot_a], send.at[0])
    local_b = pltpu.make_async_copy(mine_ref.at[1], out_ref.at[1, slot_b], send.at[1])
    local.start()
    local_b.start()
    greet([other] + along_x + along_y + along_z)
    local.wait()
    local_b.wait()
    count = [2]

    def push(step, start, size, peers):
        copies = []
        for peer in peers:
            i = count[0]
            count[0] += 1
            part = out_ref.at[step, pl.ds(start, size)]
            copy = pltpu.make_async_remote_copy(
                src_ref=part, dst_ref=part, send_sem=send.at[i], recv_sem=recv.at[i], device_id=peer, device_id_type=MESH
            )
            copy.start()
            copies.append(copy)
        return copies

    base = core * half
    first_a = push(0, base + (y * NZ + z) * NX + x, 1, along_x)
    first_b = push(1, base + (x * NZ + z) * NY + y, 1, along_y)
    for copy in first_a:
        copy.wait_recv()
    second_a = push(0, base + (y * NZ + z) * NX, NX, along_z)
    for copy in first_b:
        copy.wait_recv()
    second_b = push(1, base + (x * NZ + z) * NY, NY, along_z)
    for copy in second_a:
        copy.wait_recv()
    third_a = push(0, base + y * NZ * NX, NZ * NX, along_y)
    for copy in second_b:
        copy.wait_recv()
    third_b = push(1, base + x * NZ * NY, NZ * NY, along_x)
    for copy in third_a:
        copy.wait_recv()
    last_a = push(0, base, half, [other])
    for copy in third_b:
        copy.wait_recv()
    last_b = push(1, base, half, [other])
    for copy in last_a + last_b:
        copy.wait_recv()
    for copy in first_a + first_b + second_a + second_b + third_a + third_b + last_a + last_b:
        copy.wait_send()


def gather_rows(mine):
    copies = 2 + 2 * (3 + 7 + 3 + 1)
    return pl.pallas_call(
        gather_kernel,
        out_shape=jax.ShapeDtypeStruct((2, 256, 8, 128), BF16),
        in_specs=[pl.BlockSpec(memory_space=pltpu.VMEM)],
        out_specs=pl.BlockSpec(memory_space=pltpu.VMEM),
        scratch_shapes=[pltpu.SemaphoreType.DMA((copies,)), pltpu.SemaphoreType.DMA((copies,))],
        compiler_params=pltpu.CompilerParams(collective_id=0, has_side_effects=True),
        name="gather_rows",
    )(mine)


LEAD = 16


def split(v):
    high = v.astype(BF16)
    return high, (v - high.astype(F32)).astype(BF16)


def similar_kernel(targets_ref, rows_ref, emb_ref, high_ref, low_ref, gram_ref, block_ref, r_ref, wide_ref, chosen_ref, norm_ref, own_ref):
    step = pl.program_id(0)

    @pl.when(step == 0)
    def _():
        for s in range(2):
            slot = lax.broadcasted_iota(jnp.int32, (256, 256), 0)
            pick = jnp.where(slot == targets_ref[s : s + 1, :], 1.0, 0.0).astype(BF16)
            wide_ref[...] = rows_ref[s].reshape(2048, 128).astype(F32)
            for q in range(8):
                part = wide_ref[pl.ds(q, 256, stride=8), :].astype(BF16)
                chosen_ref[256 * s : 256 * s + 256, 128 * q : 128 * q + 128] = dot(pick, part, (0, 0)).astype(BF16)
        dots = dot(chosen_ref[...], chosen_ref[...], (1, 1))
        row = lax.broadcasted_iota(jnp.int32, (512, 512), 0)
        col = lax.broadcasted_iota(jnp.int32, (512, 512), 1)
        own = jnp.where(row == col, dots, 0.0)
        norm_row = jnp.sum(own, axis=0, keepdims=True)
        norm_ref[...] = norm_row
        block = dots / (jnp.sum(own, axis=1, keepdims=True) + norm_row - dots)
        block_ref[...] = block
        lead = jnp.sum(jnp.where(col < LEAD, block, 0.0), axis=1, keepdims=True) * (1.0 / LEAD)
        use = (row >= LEAD) & (row != col)
        above = jnp.sum(jnp.where(use, block * lead, 0.0), axis=0, keepdims=True)
        below = jnp.sum(jnp.where(use, lead * lead, 0.0), axis=0, keepdims=True)
        ratio = above / jnp.where(below > 0.0, below, 1.0)
        ratio = jnp.where(below > 0.0, jnp.clip(ratio, -4.0, 4.0), 0.0)
        r_ref[...] = jnp.where(lax.broadcasted_iota(jnp.int32, (1, 512), 1) < LEAD, 0.0, ratio)
        gram_ref[...] = jnp.zeros_like(gram_ref)
        own_ref[...] = jnp.zeros_like(own_ref)

    emb = emb_ref[...]
    wide = emb.astype(F32)
    norms = jnp.sum(wide * wide, axis=1, keepdims=True)
    dots = dot(emb, chosen_ref[...], (1, 1))
    similar = dots / (norms + norm_ref[...] - dots)
    lane = lax.broadcasted_iota(jnp.int32, (TILE, 128), 1)
    lead = jnp.sum(jnp.where(lane < LEAD, similar[:, :128], 0.0), axis=1, keepdims=True) * (1.0 / LEAD)
    similar = similar - lead * r_ref[...]
    high, low = split(similar)
    high_ref[...] = high
    low_ref[...] = low
    own_ref[...] += jnp.sum(low.astype(F32) * low.astype(F32), axis=0, keepdims=True)
    for b, (i, j) in enumerate(UPPER):
        if i == j:
            left_high, left_low = high[:, 128 * i : 128 * i + 128], low[:, 128 * i : 128 * i + 128]
            part = dot(left_high, high[:, 128 * i :], (0, 0))
            part += dot(left_high, low[:, 128 * i :], (0, 0)) + dot(left_low, high[:, 128 * i :], (0, 0))
            for e in range(4 - i):
                gram_ref[b + e] += part[:, 128 * e : 128 * e + 128]

    @pl.when(step == pl.num_programs(0) - 1)
    def _():
        row = lax.broadcasted_iota(jnp.int32, (128, 128), 0)
        col = lax.broadcasted_iota(jnp.int32, (128, 128), 1)
        for b, (i, j) in enumerate(UPPER):
            if i == j:
                gram_ref[b] += jnp.where(row == col, own_ref[:, 128 * i : 128 * i + 128], 0.0)


def similar_call(targets, rows, embeddings):
    count = embeddings.shape[0] // TILE
    whole = lambda shape: pl.BlockSpec(shape, lambda i: (0,) * len(shape))
    tile = lambda width: pl.BlockSpec((TILE, width), lambda i: (i, 0))
    return pl.pallas_call(
        similar_kernel,
        grid=(count,),
        out_shape=(
            jax.ShapeDtypeStruct((embeddings.shape[0], 512), BF16),
            jax.ShapeDtypeStruct((embeddings.shape[0], 512), BF16),
            jax.ShapeDtypeStruct((10, 128, 128), F32),
            jax.ShapeDtypeStruct((512, 512), F32),
            jax.ShapeDtypeStruct((1, 512), F32),
        ),
        in_specs=[whole((2, 256)), whole((2, 256, 8, 128)), tile(1024)],
        out_specs=(tile(512), tile(512), whole((10, 128, 128)), whole((512, 512)), whole((1, 512))),
        scratch_shapes=[
            pltpu.VMEM((2048, 128), F32),
            pltpu.VMEM((512, 1024), BF16),
            pltpu.VMEM((1, 512), F32),
            pltpu.VMEM((1, 512), F32),
        ],
        compiler_params=pltpu.CompilerParams(vmem_limit_bytes=56 << 20, dimension_semantics=("arbitrary",)),
        name="similar",
    )(targets, rows, embeddings)


STREAMS = ((0, 384), (384, 256))


def reduce_kernel(in_ref, block_ref, r_ref, out_ref, tail_ref, w_ref, diag_ref, core_in, big_in, small_in, z_in, half_sum, big_sum, small_sum, send, recv):
    x, y, z, core = coords()
    other = (lax.axis_index("bank"), 1 - core)
    along_x, along_y, along_z = axis_peers(x, y, z, core)
    greet([other] + along_x + along_y + along_z)
    count = [0]
    everything = []

    def push(src, dst, peer):
        i = count[0]
        count[0] += 1
        copy = pltpu.make_async_remote_copy(
            src_ref=src, dst_ref=dst, send_sem=send.at[i], recv_sem=recv.at[i], device_id=peer, device_id_type=MESH
        )
        copy.start()
        everything.append(copy)
        return copy

    w_ref[...] = block_ref[...]
    work = cholesky_steps(w_ref, diag_ref)
    mine = core * 640
    theirs = (1 - core) * 640
    axes = ((along_x, NX, x), (along_y, NY, y))
    state = []
    for s, (start, size) in enumerate(STREAMS):
        state.append(push(in_ref.at[pl.ds(theirs + start, size)], core_in.at[pl.ds(start, size)], other))
    big = []
    for s, (start, size) in enumerate(STREAMS):
        peers, n, pos = axes[s]
        next(work)
        state[s].wait_recv()
        half_sum[pl.ds(start, size), :] = in_ref[pl.ds(mine + start, size), :] + core_in[pl.ds(start, size), :]
        part = size // 4
        copies = []
        for o in range(1, n):
            to = lax.rem(pos + o, n)
            copies.append(
                push(
                    half_sum.at[pl.ds(start + to * part, part)],
                    big_in.at[o - 1, pl.ds(start // 4, part)],
                    peers[o - 1],
                )
            )
        big.append(copies)
    small = []
    for s, (start, size) in enumerate(STREAMS):
        _, n, pos = axes[s]
        peers, n2, pos2 = axes[1 - s]
        part = size // 4
        next(work)
        for copy in big[s]:
            copy.wait_recv()
        total = half_sum[pl.ds(start + pos * part, part), :]
        for o in range(n - 1):
            total = total + big_in[o, start // 4 : start // 4 + part, :]
        big_sum[start // 4 : start // 4 + part, :] = total
        tiny = part // 4
        copies = []
        for o in range(1, n2):
            to = lax.rem(pos2 + o, n2)
            copies.append(
                push(
                    big_sum.at[pl.ds(start // 4 + to * tiny, tiny)],
                    small_in.at[o - 1, pl.ds(start // 16, tiny)],
                    peers[o - 1],
                )
            )
        small.append(copies)
    last = []
    for s, (start, size) in enumerate(STREAMS):
        _, n2, pos2 = axes[1 - s]
        tiny = size // 16
        next(work)
        for copy in small[s]:
            copy.wait_recv()
        total = big_sum[pl.ds(start // 4 + pos2 * tiny, tiny), :]
        for o in range(n2 - 1):
            total = total + small_in[o, start // 16 : start // 16 + tiny, :]
        small_sum[start // 16 : start // 16 + tiny, :] = total
        piece = small_sum.at[pl.ds(start // 16, tiny)]
        last.append([push(piece, z_in.at[z, pl.ds(start // 16, tiny)], peer) for peer in along_z])
        z_in[z, start // 16 : start // 16 + tiny, :] = total
    back = []
    for s, (start, size) in enumerate(STREAMS):
        _, n, pos = axes[s]
        peers, n2, pos2 = axes[1 - s]
        part, tiny = size // 4, size // 16
        next(work)
        for copy in last[s]:
            copy.wait_recv()
        total = z_in[0, start // 16 : start // 16 + tiny, :]
        for o in range(1, NZ):
            total = total + z_in[o, start // 16 : start // 16 + tiny, :]
        at = mine + start + pos * part + pos2 * tiny
        out_ref[pl.ds(at, tiny), :] = total
        piece = out_ref.at[pl.ds(at, tiny)]
        back.append([push(piece, piece, peer) for peer in peers])
    far = []
    for s, (start, size) in enumerate(STREAMS):
        peers, n, pos = axes[s]
        part = size // 4
        next(work)
        for copy in back[s]:
            copy.wait_recv()
        piece = out_ref.at[pl.ds(mine + start + pos * part, part)]
        far.append([push(piece, piece, peer) for peer in peers])
    final = []
    for s, (start, size) in enumerate(STREAMS):
        next(work)
        for copy in far[s]:
            copy.wait_recv()
        piece = out_ref.at[pl.ds(mine + start, size)]
        final.append(push(piece, piece, other))
    for _ in work:
        pass
    inverse = lower_blocks(w_ref[...])
    weight = jnp.sum(inverse * r_ref[...], axis=1, keepdims=True) * (1.0 / LEAD)
    tail_ref[...] = inverse + jnp.where(lax.broadcasted_iota(jnp.int32, (512, 512), 1) < LEAD, weight, 0.0)
    for copy in final:
        copy.wait_recv()
    for copy in everything:
        copy.wait_send()


def reduce_gram(gram, block, ratio):
    copies = 2 * (1 + 3 + 3 + 7 + 3 + 3 + 1)
    total, tail = pl.pallas_call(
        reduce_kernel,
        out_shape=(jax.ShapeDtypeStruct((1280, 128), F32), jax.ShapeDtypeStruct((512, 512), F32)),
        in_specs=[pl.BlockSpec(memory_space=pltpu.VMEM)] * 3,
        out_specs=(pl.BlockSpec(memory_space=pltpu.VMEM),) * 2,
        scratch_shapes=[
            pltpu.VMEM((512, 512), F32),
            pltpu.VMEM((8, NB, 128), F32),
            pltpu.VMEM((640, 128), F32),
            pltpu.VMEM((3, 160, 128), F32),
            pltpu.VMEM((3, 40, 128), F32),
            pltpu.VMEM((NZ, 40, 128), F32),
            pltpu.VMEM((640, 128), F32),
            pltpu.VMEM((160, 128), F32),
            pltpu.VMEM((40, 128), F32),
            pltpu.SemaphoreType.DMA((copies,)),
            pltpu.SemaphoreType.DMA((copies,)),
        ],
        compiler_params=pltpu.CompilerParams(collective_id=1, has_side_effects=True, vmem_limit_bytes=48 << 20),
        name="reduce_gram",
    )(gram.reshape(1280, 128), block, ratio)
    return total.reshape(10, 128, 128), tail


def basis_kernel(total_rows, gram_ref, tail_ref, high_ref, low_ref, basis_ref, triangle_ref, w_ref, diag_ref, inv_high, inv_low):
    @pl.when(pl.program_id(0) == 0)
    def _():
        for b, (i, j) in enumerate(UPPER):
            w_ref[128 * i : 128 * i + 128, 128 * j : 128 * j + 128] = gram_ref[b] / total_rows
        cholesky_inverse(w_ref, diag_ref)
        w = w_ref[...]
        inv_high[...], inv_low[...] = split(lower_blocks(w))
        row = lax.broadcasted_iota(jnp.int32, (512, 512), 0)
        col = lax.broadcasted_iota(jnp.int32, (512, 512), 1)
        w_ref[...] = jnp.where(row < col, w, 0.0)
        lane = lax.broadcasted_iota(jnp.int32, (NB, 128), 1)
        sub = lax.broadcasted_iota(jnp.int32, (NB, 128), 0)
        for k in range(8):
            left = 128 * (k // 2)
            both = diag_ref[k]
            keep = w_ref[NB * k : NB * k + NB, left : left + 128]
            if k % 2:
                mine = pltpu.roll(both, 64, 1)
                keep = jnp.where(lane >= 64, jnp.where(lane - 64 >= sub, mine, 0.0), keep)
            else:
                keep = jnp.where(lane < 64, jnp.where(lane >= sub, both, 0.0), keep)
            w_ref[NB * k : NB * k + NB, left : left + 128] = keep
        triangle_ref[...] = dot(w_ref[...], tail_ref[...], (1, 1), HI)

    high, low = high_ref[...], low_ref[...]
    for start, depth in ((0, 256), (256, 512)):
        right_high, right_low = inv_high[start : start + 256, :depth], inv_low[start : start + 256, :depth]
        out = dot(low[:, :depth], right_high, (1, 1)) + dot(high[:, :depth], right_low, (1, 1))
        basis_ref[:, start : start + 256] = out + dot(high[:, :depth], right_high, (1, 1))


def basis_call(gram, tail, high, low, total_rows):
    count = high.shape[0] // TILE
    whole = lambda shape: pl.BlockSpec(shape, lambda i: (0,) * len(shape))
    tile = pl.BlockSpec((TILE, 512), lambda i: (i, 0))
    return pl.pallas_call(
        functools.partial(basis_kernel, total_rows),
        grid=(count,),
        out_shape=(jax.ShapeDtypeStruct(high.shape, F32), jax.ShapeDtypeStruct((512, 512), F32)),
        in_specs=[whole((10, 128, 128)), whole((512, 512)), tile, tile],
        out_specs=(tile, whole((512, 512))),
        scratch_shapes=[
            pltpu.VMEM((512, 512), F32),
            pltpu.VMEM((8, NB, 128), F32),
            pltpu.VMEM((512, 512), BF16),
            pltpu.VMEM((512, 512), BF16),
        ],
        compiler_params=pltpu.CompilerParams(vmem_limit_bytes=56 << 20, dimension_semantics=("arbitrary",)),
        name="basis",
    )(gram, tail, high, low)


def pick_kernel(row_count, pivots_ref, emb_ref, mine_ref, targets_ref, block_ref, sems):
    start = (lax.axis_index("bank") * 2 + lax.axis_index("sub")) * row_count
    pivots = pivots_ref[...]
    inside = (pivots >= start) & (pivots < start + row_count)
    copies, offsets = [], []
    for s in range(2):
        local = jnp.sum(jnp.where(inside[s : s + 1], pivots[s : s + 1] - start, 0))
        first = pl.multiple_of((local // 16) * 16, 16)
        copy = pltpu.make_async_copy(emb_ref.at[pl.ds(first, 16)], block_ref.at[s], sems.at[s])
        copy.start()
        copies.append(copy)
        offsets.append(local - first)
    owner = jnp.floor((pivots.astype(F32) + 0.5) * (1.0 / row_count)).astype(jnp.int32)
    bank, core = owner >> 1, owner & 1
    bx, bz, by = bank & (NX - 1), (bank >> 2) & (NZ - 1), bank >> 5
    first = core * 128 + bank
    second = core * 128 + (bx * NZ + bz) * NY + by
    targets_ref[...] = jnp.where(lax.broadcasted_iota(jnp.int32, (2, 256), 0) == 0, first, second)
    for s in range(2):
        copies[s].wait()
        rows = block_ref[s].astype(F32)
        keep = lax.broadcasted_iota(jnp.int32, (16, 1024), 0) == offsets[s]
        row = jnp.sum(jnp.where(keep, rows, 0.0), axis=0, keepdims=True)
        mine_ref[s] = jnp.concatenate([row[:, 128 * q : 128 * q + 128] for q in range(8)], axis=0).astype(BF16)


def pick_rows(pivots, embeddings):
    return pl.pallas_call(
        functools.partial(pick_kernel, embeddings.shape[0]),
        out_shape=(jax.ShapeDtypeStruct((2, 8, 128), BF16), jax.ShapeDtypeStruct((2, 256), jnp.int32)),
        in_specs=[pl.BlockSpec(memory_space=pltpu.VMEM), pl.BlockSpec(memory_space=pl.ANY)],
        out_specs=(pl.BlockSpec(memory_space=pltpu.VMEM),) * 2,
        scratch_shapes=[pltpu.VMEM((2, 16, 1024), BF16), pltpu.SemaphoreType.DMA((2,))],
        name="pick_rows",
    )(pivots, embeddings)


def per_device(embeddings, pivots):
    total_rows = embeddings.shape[0] * lax.axis_size(("bank", "sub"))
    mine, targets = pick_rows(pivots, embeddings)
    rows = gather_rows(mine)
    high, low, gram, block, ratio = similar_call(targets, rows, embeddings)
    gram, tail = reduce_gram(gram, block, ratio)
    return basis_call(gram, tail, high, low, float(total_rows))


def solution(mesh):
    in_specs = (P(("bank", "sub"), None), P())
    out_specs = (P(("bank", "sub"), None), P())
    return jax.shard_map(per_device, mesh=mesh, in_specs=in_specs, out_specs=out_specs, check_vma=False)
```

```python
import functools

import jax
import jax.numpy as jnp
from jax import lax
from jax.experimental import pallas as pl
from jax.experimental.pallas import tpu as pltpu
from jax.sharding import PartitionSpec as P

HI = lax.Precision.HIGHEST
F32 = jnp.float32
BF16 = jnp.bfloat16
P_SIZE = 256
NX, NY, NZ = 4, 4, 8
NB = 64
TILE = 512
UPPER = [(i, j) for i in range(4) for j in range(i, 4)]
MESH = pl.DeviceIdType.MESH


def dot(a, b, dims, precision=None):
    return lax.dot_general(a, b, ((dims[:1], dims[1:]), ((), ())), precision=precision, preferred_element_type=F32)


def base_block(rows):
    count = NB // 8
    rows = list(rows)
    sub = lax.broadcasted_iota(jnp.int32, (8, 128), 0)
    lane = lax.broadcasted_iota(jnp.int32, (8, 128), 1)
    full = lambda v: jnp.broadcast_to(v, (8, 128))

    def fetch(k):
        spread = lambda v, j: full(jnp.sum(jnp.where(lane == j, v, 0.0), axis=1, keepdims=True))
        return {t: [spread(rows[t], 8 * k + c) for c in range(8)] for t in range(k, count)}

    out = []
    now = fetch(0)
    for k in range(count):
        later = fetch(k + 1) if k + 1 < count else None
        scale = jnp.zeros((8, 128), F32)
        for c in range(8):
            pivot = full(now[k][c][c : c + 1, :])
            pivot_row = full(rows[k][c : c + 1, :])
            ahead = [full(now[k][e][c : c + 1, :]) for e in range(c + 1, 8)]
            if later is not None:
                beyond = [full(now[k + 1][c][e : e + 1, :]) for e in range(8)]
            inverse = 1.0 / pivot
            scale = jnp.where(sub == c, pivot, scale)
            for t in range(k, count):
                column = jnp.where(sub > c, now[t][c], 0.0) if t == k else now[t][c]
                mult = column * inverse
                rows[t] = rows[t] - mult * pivot_row
                for e in range(c + 1, 8):
                    now[t][e] = now[t][e] - mult * ahead[e - c - 1]
                if t > k:
                    for e in range(8):
                        later[t][e] = later[t][e] - mult * beyond[e]
        out.append(rows[k] * lax.rsqrt(scale))
        now = later
    return out


def cholesky_steps(w_ref, diag_ref):
    n = w_ref.shape[0]
    lane = lax.broadcasted_iota(jnp.int32, (8, 128), 1)
    sub = lax.broadcasted_iota(jnp.int32, (8, 128), 0)
    block = w_ref[0:NB, 0:128]
    for k in range(n // NB):
        r0, r1 = k * NB, k * NB + NB
        rows = []
        for t in range(NB // 8):
            eye = jnp.where(lane - NB == sub + 8 * t, 1.0, 0.0)
            rows.append(jnp.where(lane < NB, block[8 * t : 8 * t + 8, :], eye))
        both = jnp.concatenate(base_block(rows), axis=0)
        diag_ref[k] = both
        inverse = both[:, NB:]
        if r1 < n:
            left = (r1 // 128) * 128
            ahead, block = w_ref[r0:r1, left : left + 128], w_ref[r1 : r1 + NB, left : left + 128]
            if r1 % 128:
                ahead, block = pltpu.roll(ahead, NB, 1), pltpu.roll(block, NB, 1)
            ahead = dot(inverse, ahead, (1, 0), HI)
            block = block - dot(ahead[:, :NB], ahead, (0, 0), HI)
        yield
        wide = w_ref[r0:r1, :]
        col = lax.broadcasted_iota(jnp.int32, (NB, n), 1)
        row = lax.broadcasted_iota(jnp.int32, (NB, n), 0)
        wide = jnp.where((col >= r0) & (col < r1), jnp.where(col - r0 == row, 1.0, 0.0), wide)
        strip = dot(inverse, wide, (1, 0), HI)
        w_ref[r0:r1, :] = strip
        if r1 < n:
            update = dot(strip[:, r1:], strip, (0, 0), HI)
            current = w_ref[r1:, :]
            col = lax.broadcasted_iota(jnp.int32, (n - r1, n), 1)
            w_ref[r1:, :] = jnp.where((col >= r0) & (col < r1), 0.0, current) - update


def cholesky_inverse(w_ref, diag_ref):
    for _ in cholesky_steps(w_ref, diag_ref):
        pass


def lower_blocks(w):
    n = w.shape[0]
    row = lax.broadcasted_iota(jnp.int32, (n, n), 0)
    col = lax.broadcasted_iota(jnp.int32, (n, n), 1)
    return jnp.where(row >= col, w, 0.0)


def coords():
    bank = lax.axis_index("bank")
    core = lax.axis_index("sub")
    x = lax.rem(bank, NX)
    z = lax.rem(bank // NX, NZ)
    y = bank // (NX * NZ)
    return x, y, z, core


def bank_of(x, y, z):
    return (y * NZ + z) * NX + x


def greet(peers):
    barrier = pltpu.get_barrier_semaphore()
    for peer in peers:
        pl.semaphore_signal(barrier, inc=1, device_id=peer, device_id_type=MESH)
    pl.semaphore_wait(barrier, len(peers))


def axis_peers(x, y, z, core):
    along_x = [(bank_of(lax.rem(x + o, NX), y, z), core) for o in range(1, NX)]
    along_y = [(bank_of(x, lax.rem(y + o, NY), z), core) for o in range(1, NY)]
    along_z = [(bank_of(x, y, lax.rem(z + o, NZ)), core) for o in range(1, NZ)]
    return along_x, along_y, along_z


def gather_kernel(mine_ref, out_ref, send, recv):
    x, y, z, core = coords()
    other = (lax.axis_index("bank"), 1 - core)
    along_x, along_y, along_z = axis_peers(x, y, z, core)
    half = NX * NY * NZ
    slot_a = core * half + (y * NX + x) * NZ + z
    slot_b = core * half + (x * NY + y) * NZ + z
    local = pltpu.make_async_copy(mine_ref.at[0], out_ref.at[0, slot_a], send.at[0])
    local_b = pltpu.make_async_copy(mine_ref.at[1], out_ref.at[1, slot_b], send.at[1])
    local.start()
    local_b.start()
    greet([other] + along_x + along_y + along_z)
    local.wait()
    local_b.wait()
    count = [2]

    def push(step, start, size, peers):
        copies = []
        for peer in peers:
            i = count[0]
            count[0] += 1
            part = out_ref.at[step, pl.ds(start, size)]
            copy = pltpu.make_async_remote_copy(
                src_ref=part, dst_ref=part, send_sem=send.at[i], recv_sem=recv.at[i], device_id=peer, device_id_type=MESH
            )
            copy.start()
            copies.append(copy)
        return copies

    base = core * half
    first_a = push(0, slot_a, 1, along_z)
    first_b = push(1, slot_b, 1, along_z)
    for copy in first_a:
        copy.wait_recv()
    second_a = push(0, slot_a - z, NZ, along_x)
    for copy in first_b:
        copy.wait_recv()
    second_b = push(1, slot_b - z, NZ, along_y)
    for copy in second_a:
        copy.wait_recv()
    third_a = push(0, base + y * NX * NZ, NX * NZ, along_y)
    for copy in second_b:
        copy.wait_recv()
    third_b = push(1, base + x * NY * NZ, NY * NZ, along_x)
    for copy in third_a:
        copy.wait_recv()
    last_a = push(0, base, half, [other])
    for copy in third_b:
        copy.wait_recv()
    last_b = push(1, base, half, [other])
    for copy in last_a + last_b:
        copy.wait_recv()
    for copy in first_a + first_b + second_a + second_b + third_a + third_b + last_a + last_b:
        copy.wait_send()


def gather_rows(mine):
    copies = 2 + 2 * (3 + 7 + 3 + 1)
    return pl.pallas_call(
        gather_kernel,
        out_shape=jax.ShapeDtypeStruct((2, 256, 8, 128), BF16),
        in_specs=[pl.BlockSpec(memory_space=pltpu.VMEM)],
        out_specs=pl.BlockSpec(memory_space=pltpu.VMEM),
        scratch_shapes=[pltpu.SemaphoreType.DMA((copies,)), pltpu.SemaphoreType.DMA((copies,))],
        compiler_params=pltpu.CompilerParams(collective_id=0, has_side_effects=True, vmem_limit_bytes=8 << 20),
        name="gather_rows",
    )(mine)


LEAD = 16


def split(v):
    high = v.astype(BF16)
    return high, (v - high.astype(F32)).astype(BF16)


def similar_kernel(targets_ref, rows_ref, emb_ref, high_ref, low_ref, gram_ref, block_ref, r_ref, wide_ref, chosen_ref, norm_ref, own_ref):
    step = pl.program_id(0)

    @pl.when(step == 0)
    def _():
        for s in range(2):
            slot = lax.broadcasted_iota(jnp.int32, (256, 256), 0)
            pick = jnp.where(slot == targets_ref[s : s + 1, :], 1.0, 0.0).astype(BF16)
            wide_ref[...] = rows_ref[s].reshape(2048, 128).astype(F32)
            for q in range(8):
                part = wide_ref[pl.ds(q, 256, stride=8), :].astype(BF16)
                chosen_ref[256 * s : 256 * s + 256, 128 * q : 128 * q + 128] = dot(pick, part, (0, 0)).astype(BF16)
        dots = dot(chosen_ref[...], chosen_ref[...], (1, 1))
        row = lax.broadcasted_iota(jnp.int32, (512, 512), 0)
        col = lax.broadcasted_iota(jnp.int32, (512, 512), 1)
        own = jnp.where(row == col, dots, 0.0)
        norm_row = jnp.sum(own, axis=0, keepdims=True)
        norm_ref[...] = norm_row
        block = dots / (jnp.sum(own, axis=1, keepdims=True) + norm_row - dots)
        block_ref[...] = block
        lead = jnp.sum(jnp.where(col < LEAD, block, 0.0), axis=1, keepdims=True) * (1.0 / LEAD)
        use = (row >= LEAD) & (row != col)
        above = jnp.sum(jnp.where(use, block * lead, 0.0), axis=0, keepdims=True)
        below = jnp.sum(jnp.where(use, lead * lead, 0.0), axis=0, keepdims=True)
        ratio = above / jnp.where(below > 0.0, below, 1.0)
        ratio = jnp.where(below > 0.0, jnp.clip(ratio, -4.0, 4.0), 0.0)
        r_ref[...] = jnp.where(lax.broadcasted_iota(jnp.int32, (1, 512), 1) < LEAD, 0.0, ratio)
        gram_ref[...] = jnp.zeros_like(gram_ref)
        own_ref[...] = jnp.zeros_like(own_ref)

    emb = emb_ref[...]
    wide = emb.astype(F32)
    norms = jnp.sum(wide * wide, axis=1, keepdims=True)
    dots = dot(emb, chosen_ref[...], (1, 1))
    similar = dots / (norms + norm_ref[...] - dots)
    lane = lax.broadcasted_iota(jnp.int32, (TILE, 128), 1)
    lead = jnp.sum(jnp.where(lane < LEAD, similar[:, :128], 0.0), axis=1, keepdims=True) * (1.0 / LEAD)
    similar = similar - lead * r_ref[...]
    high, low = split(similar)
    high_ref[...] = high
    low_ref[...] = low
    own_ref[...] += jnp.sum(low.astype(F32) * low.astype(F32), axis=0, keepdims=True)
    for b, (i, j) in enumerate(UPPER):
        if i == j:
            left_high, left_low = high[:, 128 * i : 128 * i + 128], low[:, 128 * i : 128 * i + 128]
            part = dot(left_high, high[:, 128 * i :], (0, 0))
            part += dot(left_high, low[:, 128 * i :], (0, 0)) + dot(left_low, high[:, 128 * i :], (0, 0))
            for e in range(4 - i):
                gram_ref[b + e] += part[:, 128 * e : 128 * e + 128]

    @pl.when(step == pl.num_programs(0) - 1)
    def _():
        row = lax.broadcasted_iota(jnp.int32, (128, 128), 0)
        col = lax.broadcasted_iota(jnp.int32, (128, 128), 1)
        for b, (i, j) in enumerate(UPPER):
            if i == j:
                gram_ref[b] += jnp.where(row == col, own_ref[:, 128 * i : 128 * i + 128], 0.0)


def similar_call(targets, rows, embeddings):
    count = embeddings.shape[0] // TILE
    whole = lambda shape: pl.BlockSpec(shape, lambda i: (0,) * len(shape))
    tile = lambda width: pl.BlockSpec((TILE, width), lambda i: (i, 0))
    return pl.pallas_call(
        similar_kernel,
        grid=(count,),
        out_shape=(
            jax.ShapeDtypeStruct((embeddings.shape[0], 512), BF16),
            jax.ShapeDtypeStruct((embeddings.shape[0], 512), BF16),
            jax.ShapeDtypeStruct((10, 128, 128), F32),
            jax.ShapeDtypeStruct((512, 512), F32),
            jax.ShapeDtypeStruct((1, 512), F32),
        ),
        in_specs=[whole((2, 256)), whole((2, 256, 8, 128)), tile(1024)],
        out_specs=(tile(512), tile(512), whole((10, 128, 128)), whole((512, 512)), whole((1, 512))),
        scratch_shapes=[
            pltpu.VMEM((2048, 128), F32),
            pltpu.VMEM((512, 1024), BF16),
            pltpu.VMEM((1, 512), F32),
            pltpu.VMEM((1, 512), F32),
        ],
        compiler_params=pltpu.CompilerParams(vmem_limit_bytes=24 << 20, dimension_semantics=("arbitrary",)),
        name="similar",
    )(targets, rows, embeddings)


STREAMS = ((0, 384), (384, 256))


def reduce_kernel(in_ref, block_ref, r_ref, out_ref, tail_ref, w_ref, diag_ref, core_in, big_in, small_in, z_in, half_sum, big_sum, small_sum, send, recv):
    x, y, z, core = coords()
    other = (lax.axis_index("bank"), 1 - core)
    along_x, along_y, along_z = axis_peers(x, y, z, core)
    greet([other] + along_x + along_y + along_z)
    count = [0]
    everything = []

    def push(src, dst, peer):
        i = count[0]
        count[0] += 1
        copy = pltpu.make_async_remote_copy(
            src_ref=src, dst_ref=dst, send_sem=send.at[i], recv_sem=recv.at[i], device_id=peer, device_id_type=MESH
        )
        copy.start()
        everything.append(copy)
        return copy

    w_ref[...] = block_ref[...]
    work = cholesky_steps(w_ref, diag_ref)
    mine = core * 640
    theirs = (1 - core) * 640
    axes = ((along_x, NX, x), (along_y, NY, y))
    state = []
    for s, (start, size) in enumerate(STREAMS):
        state.append(push(in_ref.at[pl.ds(theirs + start, size)], core_in.at[pl.ds(start, size)], other))
    big = []
    for s, (start, size) in enumerate(STREAMS):
        peers, n, pos = axes[s]
        next(work, None)
        state[s].wait_recv()
        half_sum[pl.ds(start, size), :] = in_ref[pl.ds(mine + start, size), :] + core_in[pl.ds(start, size), :]
        part = size // 4
        copies = []
        for o in range(1, n):
            to = lax.rem(pos + o, n)
            copies.append(
                push(
                    half_sum.at[pl.ds(start + to * part, part)],
                    big_in.at[o - 1, pl.ds(start // 4, part)],
                    peers[o - 1],
                )
            )
        big.append(copies)
    small = []
    for s, (start, size) in enumerate(STREAMS):
        _, n, pos = axes[s]
        peers, n2, pos2 = axes[1 - s]
        part = size // 4
        next(work, None)
        for copy in big[s]:
            copy.wait_recv()
        total = half_sum[pl.ds(start + pos * part, part), :]
        for o in range(n - 1):
            total = total + big_in[o, start // 4 : start // 4 + part, :]
        big_sum[start // 4 : start // 4 + part, :] = total
        tiny = part // 4
        copies = []
        for o in range(1, n2):
            to = lax.rem(pos2 + o, n2)
            copies.append(
                push(
                    big_sum.at[pl.ds(start // 4 + to * tiny, tiny)],
                    small_in.at[o - 1, pl.ds(start // 16, tiny)],
                    peers[o - 1],
                )
            )
        small.append(copies)
    last = []
    for s, (start, size) in enumerate(STREAMS):
        _, n2, pos2 = axes[1 - s]
        tiny = size // 16
        next(work, None)
        for copy in small[s]:
            copy.wait_recv()
        total = big_sum[pl.ds(start // 4 + pos2 * tiny, tiny), :]
        for o in range(n2 - 1):
            total = total + small_in[o, start // 16 : start // 16 + tiny, :]
        small_sum[start // 16 : start // 16 + tiny, :] = total
        piece = small_sum.at[pl.ds(start // 16, tiny)]
        last.append([push(piece, z_in.at[z, pl.ds(start // 16, tiny)], peer) for peer in along_z])
        z_in[z, start // 16 : start // 16 + tiny, :] = total
    back = []
    for s, (start, size) in enumerate(STREAMS):
        _, n, pos = axes[s]
        peers, n2, pos2 = axes[1 - s]
        part, tiny = size // 4, size // 16
        next(work, None)
        for copy in last[s]:
            copy.wait_recv()
        total = z_in[0, start // 16 : start // 16 + tiny, :]
        for o in range(1, NZ):
            total = total + z_in[o, start // 16 : start // 16 + tiny, :]
        at = mine + start + pos * part + pos2 * tiny
        out_ref[pl.ds(at, tiny), :] = total
        piece = out_ref.at[pl.ds(at, tiny)]
        back.append([push(piece, piece, peer) for peer in peers])
    far = []
    for s, (start, size) in enumerate(STREAMS):
        peers, n, pos = axes[s]
        part = size // 4
        next(work, None)
        for copy in back[s]:
            copy.wait_recv()
        piece = out_ref.at[pl.ds(mine + start + pos * part, part)]
        far.append([push(piece, piece, peer) for peer in peers])
    final = []
    for s, (start, size) in enumerate(STREAMS):
        next(work, None)
        for copy in far[s]:
            copy.wait_recv()
        piece = out_ref.at[pl.ds(mine + start, size)]
        final.append(push(piece, piece, other))
    for _ in work:
        pass
    inverse = lower_blocks(w_ref[...])
    weight = jnp.sum(inverse * r_ref[...], axis=1, keepdims=True) * (1.0 / LEAD)
    tail_ref[...] = inverse + jnp.where(lax.broadcasted_iota(jnp.int32, (512, 512), 1) < LEAD, weight, 0.0)
    for copy in final:
        copy.wait_recv()
    for copy in everything:
        copy.wait_send()


def reduce_gram(gram, block, ratio):
    copies = 2 * (1 + 3 + 3 + 7 + 3 + 3 + 1)
    total, tail = pl.pallas_call(
        reduce_kernel,
        out_shape=(jax.ShapeDtypeStruct((1280, 128), F32), jax.ShapeDtypeStruct((512, 512), F32)),
        in_specs=[pl.BlockSpec(memory_space=pltpu.VMEM)] * 3,
        out_specs=(pl.BlockSpec(memory_space=pltpu.VMEM),) * 2,
        scratch_shapes=[
            pltpu.VMEM((512, 512), F32),
            pltpu.VMEM((8, NB, 128), F32),
            pltpu.VMEM((640, 128), F32),
            pltpu.VMEM((3, 160, 128), F32),
            pltpu.VMEM((3, 40, 128), F32),
            pltpu.VMEM((NZ, 40, 128), F32),
            pltpu.VMEM((640, 128), F32),
            pltpu.VMEM((160, 128), F32),
            pltpu.VMEM((40, 128), F32),
            pltpu.SemaphoreType.DMA((copies,)),
            pltpu.SemaphoreType.DMA((copies,)),
        ],
        compiler_params=pltpu.CompilerParams(collective_id=1, has_side_effects=True, vmem_limit_bytes=24 << 20),
        name="reduce_gram",
    )(gram.reshape(1280, 128), block, ratio)
    return total.reshape(10, 128, 128), tail


def basis_kernel(total_rows, gram_ref, tail_ref, high_ref, low_ref, basis_ref, triangle_ref, w_ref, diag_ref, inv_high, inv_low):
    @pl.when(pl.program_id(0) == 0)
    def _():
        for b, (i, j) in enumerate(UPPER):
            w_ref[128 * i : 128 * i + 128, 128 * j : 128 * j + 128] = gram_ref[b] / total_rows
        cholesky_inverse(w_ref, diag_ref)
        w = w_ref[...]
        inv_high[...], inv_low[...] = split(lower_blocks(w))
        row = lax.broadcasted_iota(jnp.int32, (512, 512), 0)
        col = lax.broadcasted_iota(jnp.int32, (512, 512), 1)
        w_ref[...] = jnp.where(row < col, w, 0.0)
        lane = lax.broadcasted_iota(jnp.int32, (NB, 128), 1)
        sub = lax.broadcasted_iota(jnp.int32, (NB, 128), 0)
        for k in range(8):
            left = 128 * (k // 2)
            both = diag_ref[k]
            keep = w_ref[NB * k : NB * k + NB, left : left + 128]
            if k % 2:
                mine = pltpu.roll(both, 64, 1)
                keep = jnp.where(lane >= 64, jnp.where(lane - 64 >= sub, mine, 0.0), keep)
            else:
                keep = jnp.where(lane < 64, jnp.where(lane >= sub, both, 0.0), keep)
            w_ref[NB * k : NB * k + NB, left : left + 128] = keep
        triangle_ref[...] = dot(w_ref[...], tail_ref[...], (1, 1), HI)

    high, low = high_ref[...], low_ref[...]
    for start, depth in ((0, 256), (256, 512)):
        right_high, right_low = inv_high[start : start + 256, :depth], inv_low[start : start + 256, :depth]
        out = dot(low[:, :depth], right_high, (1, 1)) + dot(high[:, :depth], right_low, (1, 1))
        basis_ref[:, start : start + 256] = out + dot(high[:, :depth], right_high, (1, 1))


def basis_call(gram, tail, high, low, total_rows):
    count = high.shape[0] // TILE
    whole = lambda shape: pl.BlockSpec(shape, lambda i: (0,) * len(shape))
    tile = pl.BlockSpec((TILE, 512), lambda i: (i, 0))
    return pl.pallas_call(
        functools.partial(basis_kernel, total_rows),
        grid=(count,),
        out_shape=(jax.ShapeDtypeStruct(high.shape, F32), jax.ShapeDtypeStruct((512, 512), F32)),
        in_specs=[whole((10, 128, 128)), whole((512, 512)), tile, tile],
        out_specs=(tile, whole((512, 512))),
        scratch_shapes=[
            pltpu.VMEM((512, 512), F32),
            pltpu.VMEM((8, NB, 128), F32),
            pltpu.VMEM((512, 512), BF16),
            pltpu.VMEM((512, 512), BF16),
        ],
        compiler_params=pltpu.CompilerParams(vmem_limit_bytes=24 << 20, dimension_semantics=("arbitrary",)),
        name="basis",
    )(gram, tail, high, low)


def pick_kernel(row_count, pivots_ref, emb_ref, mine_ref, targets_ref, block_ref, sems):
    start = (lax.axis_index("bank") * 2 + lax.axis_index("sub")) * row_count
    pivots = pivots_ref[...]
    inside = (pivots >= start) & (pivots < start + row_count)
    copies, offsets = [], []
    for s in range(2):
        local = jnp.sum(jnp.where(inside[s : s + 1], pivots[s : s + 1] - start, 0))
        first = pl.multiple_of((local // 16) * 16, 16)
        copy = pltpu.make_async_copy(emb_ref.at[pl.ds(first, 16)], block_ref.at[s], sems.at[s])
        copy.start()
        copies.append(copy)
        offsets.append(local - first)
    owner = jnp.floor((pivots.astype(F32) + 0.5) * (1.0 / row_count)).astype(jnp.int32)
    bank, core = owner >> 1, owner & 1
    bx, bz, by = bank & (NX - 1), (bank >> 2) & (NZ - 1), bank >> 5
    first = core * 128 + (by * NX + bx) * NZ + bz
    second = core * 128 + (bx * NY + by) * NZ + bz
    targets_ref[...] = jnp.where(lax.broadcasted_iota(jnp.int32, (2, 256), 0) == 0, first, second)
    for s in range(2):
        copies[s].wait()
        rows = block_ref[s].astype(F32)
        keep = lax.broadcasted_iota(jnp.int32, (16, 1024), 0) == offsets[s]
        row = jnp.sum(jnp.where(keep, rows, 0.0), axis=0, keepdims=True)
        mine_ref[s] = jnp.concatenate([row[:, 128 * q : 128 * q + 128] for q in range(8)], axis=0).astype(BF16)


def pick_rows(pivots, embeddings):
    return pl.pallas_call(
        functools.partial(pick_kernel, embeddings.shape[0]),
        out_shape=(jax.ShapeDtypeStruct((2, 8, 128), BF16), jax.ShapeDtypeStruct((2, 256), jnp.int32)),
        in_specs=[pl.BlockSpec(memory_space=pltpu.VMEM), pl.BlockSpec(memory_space=pl.ANY)],
        out_specs=(pl.BlockSpec(memory_space=pltpu.VMEM),) * 2,
        scratch_shapes=[pltpu.VMEM((2, 16, 1024), BF16), pltpu.SemaphoreType.DMA((2,))],
        name="pick_rows",
    )(pivots, embeddings)


def per_device(embeddings, pivots):
    total_rows = embeddings.shape[0] * lax.axis_size(("bank", "sub"))
    mine, targets = pick_rows(pivots, embeddings)
    rows = gather_rows(mine)
    high, low, gram, block, ratio = similar_call(targets, rows, embeddings)
    gram, tail = reduce_gram(gram, block, ratio)
    return basis_call(gram, tail, high, low, float(total_rows))


def solution(mesh):
    in_specs = (P(("bank", "sub"), None), P())
    out_specs = (P(("bank", "sub"), None), P())
    return jax.shard_map(per_device, mesh=mesh, in_specs=in_specs, out_specs=out_specs, check_vma=False)
```

```python
import functools

import jax
import jax.numpy as jnp
from jax import lax
from jax.experimental import pallas as pl
from jax.experimental.pallas import tpu as pltpu
from jax.sharding import PartitionSpec as P

HI = lax.Precision.HIGHEST
F32 = jnp.float32
BF16 = jnp.bfloat16
P_SIZE = 256
NX, NY, NZ = 4, 4, 8
NB = 64
TILE = 512
UPPER = [(i, j) for i in range(4) for j in range(i, 4)]
MESH = pl.DeviceIdType.MESH


def dot(a, b, dims, precision=None):
    return lax.dot_general(a, b, ((dims[:1], dims[1:]), ((), ())), precision=precision, preferred_element_type=F32)


def base_block(rows):
    count = NB // 8
    rows = list(rows)
    sub = lax.broadcasted_iota(jnp.int32, (8, 128), 0)
    lane = lax.broadcasted_iota(jnp.int32, (8, 128), 1)
    full = lambda v: jnp.broadcast_to(v, (8, 128))

    def fetch(k):
        spread = lambda v, j: full(jnp.sum(jnp.where(lane == j, v, 0.0), axis=1, keepdims=True))
        return {t: [spread(rows[t], 8 * k + c) for c in range(8)] for t in range(k, count)}

    out = []
    now = fetch(0)
    for k in range(count):
        later = fetch(k + 1) if k + 1 < count else None
        scale = jnp.zeros((8, 128), F32)
        for c in range(8):
            pivot = full(now[k][c][c : c + 1, :])
            pivot_row = full(rows[k][c : c + 1, :])
            ahead = [full(now[k][e][c : c + 1, :]) for e in range(c + 1, 8)]
            if later is not None:
                beyond = [full(now[k + 1][c][e : e + 1, :]) for e in range(8)]
            inverse = 1.0 / pivot
            scale = jnp.where(sub == c, pivot, scale)
            for t in range(k, count):
                column = jnp.where(sub > c, now[t][c], 0.0) if t == k else now[t][c]
                mult = column * inverse
                rows[t] = rows[t] - mult * pivot_row
                for e in range(c + 1, 8):
                    now[t][e] = now[t][e] - mult * ahead[e - c - 1]
                if t > k:
                    for e in range(8):
                        later[t][e] = later[t][e] - mult * beyond[e]
        out.append(rows[k] * lax.rsqrt(scale))
        now = later
    return out


def cholesky_steps(w_ref, diag_ref):
    n = w_ref.shape[0]
    lane = lax.broadcasted_iota(jnp.int32, (8, 128), 1)
    sub = lax.broadcasted_iota(jnp.int32, (8, 128), 0)
    block = w_ref[0:NB, 0:128]
    for k in range(n // NB):
        r0, r1 = k * NB, k * NB + NB
        rows = []
        for t in range(NB // 8):
            eye = jnp.where(lane - NB == sub + 8 * t, 1.0, 0.0)
            rows.append(jnp.where(lane < NB, block[8 * t : 8 * t + 8, :], eye))
        both = jnp.concatenate(base_block(rows), axis=0)
        diag_ref[k] = both
        inverse = both[:, NB:]
        if r1 < n:
            left = (r1 // 128) * 128
            ahead, block = w_ref[r0:r1, left : left + 128], w_ref[r1 : r1 + NB, left : left + 128]
            if r1 % 128:
                ahead, block = pltpu.roll(ahead, NB, 1), pltpu.roll(block, NB, 1)
            ahead = dot(inverse, ahead, (1, 0), HI)
            block = block - dot(ahead[:, :NB], ahead, (0, 0), HI)
        yield
        wide = w_ref[r0:r1, :]
        col = lax.broadcasted_iota(jnp.int32, (NB, n), 1)
        row = lax.broadcasted_iota(jnp.int32, (NB, n), 0)
        wide = jnp.where((col >= r0) & (col < r1), jnp.where(col - r0 == row, 1.0, 0.0), wide)
        strip = dot(inverse, wide, (1, 0), HI)
        w_ref[r0:r1, :] = strip
        if r1 < n:
            update = dot(strip[:, r1:], strip, (0, 0), HI)
            current = w_ref[r1:, :]
            col = lax.broadcasted_iota(jnp.int32, (n - r1, n), 1)
            w_ref[r1:, :] = jnp.where((col >= r0) & (col < r1), 0.0, current) - update


def cholesky_inverse(w_ref, diag_ref):
    for _ in cholesky_steps(w_ref, diag_ref):
        pass


def lower_blocks(w):
    n = w.shape[0]
    row = lax.broadcasted_iota(jnp.int32, (n, n), 0)
    col = lax.broadcasted_iota(jnp.int32, (n, n), 1)
    return jnp.where(row >= col, w, 0.0)


def coords():
    bank = lax.axis_index("bank")
    core = lax.axis_index("sub")
    x = lax.rem(bank, NX)
    z = lax.rem(bank // NX, NZ)
    y = bank // (NX * NZ)
    return x, y, z, core


def bank_of(x, y, z):
    return (y * NZ + z) * NX + x


def axis_peers(x, y, z, core):
    along_x = [(bank_of(lax.rem(x + o, NX), y, z), core) for o in range(1, NX)]
    along_y = [(bank_of(x, lax.rem(y + o, NY), z), core) for o in range(1, NY)]
    along_z = [(bank_of(x, y, lax.rem(z + o, NZ)), core) for o in range(1, NZ)]
    return along_x, along_y, along_z


LEAD = 16
STREAMS = ((0, 384), (384, 256))


def split(v):
    high = v.astype(BF16)
    return high, (v - high.astype(F32)).astype(BF16)


def gram_kernel(
    mine_hbm, targets_hbm, emb_hbm, high_hbm, low_hbm, out_ref, tail_ref,
    high_ref, low_ref, targets_ref, emb_ref, norms_ref, rows_ref, wide_ref, chosen_ref, norm_ref, r_ref, own_ref, in_ref, w_ref, diag_ref,
    core_in, big_in, small_in, z_in, half_sum, big_sum, small_sum, load, send, recv,
):
    x, y, z, core = coords()
    other = (lax.axis_index("bank"), 1 - core)
    along_x, along_y, along_z = axis_peers(x, y, z, core)
    row_count = emb_hbm.shape[0]
    tiles = row_count // TILE
    everything = []
    count = [2]

    def push(src, dst, peer):
        i = count[0]
        count[0] += 1
        copy = pltpu.make_async_remote_copy(
            src_ref=src, dst_ref=dst, send_sem=send.at[i], recv_sem=recv.at[i], device_id=peer, device_id_type=MESH
        )
        copy.start()
        everything.append(copy)
        return copy

    def arrive(copies):
        for copy in copies:
            copy.wait_recv()

    half = NX * NY * NZ
    base = core * half
    slot_a = base + (y * NX + x) * NZ + z
    slot_b = base + (x * NY + y) * NZ + z
    loads = [
        pltpu.make_async_copy(emb_hbm.at[pl.ds(t * TILE, TILE)], emb_ref.at[pl.ds(t * TILE, TILE)], load.at[t])
        for t in range(tiles)
    ]
    local = [
        pltpu.make_async_copy(mine_hbm.at[0], rows_ref.at[0, slot_a], send.at[0]),
        pltpu.make_async_copy(mine_hbm.at[1], rows_ref.at[1, slot_b], send.at[1]),
        pltpu.make_async_copy(targets_hbm, targets_ref, load.at[tiles]),
    ]
    for copy in local + loads:
        copy.start()
    peers = [other] + along_x + along_y + along_z
    barrier = pltpu.get_barrier_semaphore()
    for peer in peers:
        pl.semaphore_signal(barrier, inc=1, device_id=peer, device_id_type=MESH)

    def norms(first, last):
        for t in range(first, last):
            loads[t].wait()

        def body(i, carry):
            at = pl.ds(pl.multiple_of(i * 64, 64), 64)
            wide = emb_ref[at, :].astype(F32)
            norms_ref[at, :] = jnp.sum(wide * wide, axis=1, keepdims=True)
            return carry

        lax.fori_loop(first * (TILE // 64), last * (TILE // 64), body, 0)

    def share(step, start, size, to):
        part = rows_ref.at[step, pl.ds(start, size)]
        return [push(part, part, peer) for peer in to]

    for copy in local:
        copy.wait()
    pl.semaphore_wait(barrier, len(peers))
    first_a = share(0, slot_a, 1, along_z)
    first_b = share(1, slot_b, 1, along_z)
    norms(0, 2)
    arrive(first_a)
    second_a = share(0, slot_a - z, NZ, along_x)
    arrive(first_b)
    second_b = share(1, slot_b - z, NZ, along_y)
    norms(2, 4)
    arrive(second_a)
    third_a = share(0, base + y * NX * NZ, NX * NZ, along_y)
    arrive(second_b)
    third_b = share(1, base + x * NY * NZ, NY * NZ, along_x)
    norms(4, tiles)
    arrive(third_a)
    last_a = share(0, base, half, [other])
    arrive(third_b)
    last_b = share(1, base, half, [other])

    for s, copies in ((0, last_a), (1, last_b)):
        slot = lax.broadcasted_iota(jnp.int32, (256, 256), 0)
        pick = jnp.where(slot == targets_ref[s : s + 1, :], 1.0, 0.0).astype(BF16)
        arrive(copies)
        wide_ref[...] = rows_ref[s].reshape(2048, 128).astype(F32)
        for q in range(8):
            part = wide_ref[pl.ds(q, 256, stride=8), :].astype(BF16)
            chosen_ref[256 * s : 256 * s + 256, 128 * q : 128 * q + 128] = dot(pick, part, (0, 0)).astype(BF16)
    dots = dot(chosen_ref[...], chosen_ref[...], (1, 1))
    row = lax.broadcasted_iota(jnp.int32, (512, 512), 0)
    col = lax.broadcasted_iota(jnp.int32, (512, 512), 1)
    own = jnp.where(row == col, dots, 0.0)
    norm_row = jnp.sum(own, axis=0, keepdims=True)
    norm_ref[...] = norm_row
    block = dots / (jnp.sum(own, axis=1, keepdims=True) + norm_row - dots)
    w_ref[...] = block
    lead = jnp.sum(jnp.where(col < LEAD, block, 0.0), axis=1, keepdims=True) * (1.0 / LEAD)
    use = (row >= LEAD) & (row != col)
    above = jnp.sum(jnp.where(use, block * lead, 0.0), axis=0, keepdims=True)
    below = jnp.sum(jnp.where(use, lead * lead, 0.0), axis=0, keepdims=True)
    ratio = above / jnp.where(below > 0.0, below, 1.0)
    ratio = jnp.where(below > 0.0, jnp.clip(ratio, -4.0, 4.0), 0.0)
    r_ref[...] = jnp.where(lax.broadcasted_iota(jnp.int32, (1, 512), 1) < LEAD, 0.0, ratio)
    in_ref[...] = jnp.zeros_like(in_ref)
    own_ref[...] = jnp.zeros_like(own_ref)

    def tile(t, carry):
        at = pl.ds(pl.multiple_of(t * TILE, TILE), TILE)
        dots = dot(emb_ref[at, :], chosen_ref[...], (1, 1))
        similar = dots / (norms_ref[at, :] + norm_ref[...] - dots)
        lane = lax.broadcasted_iota(jnp.int32, (TILE, 128), 1)
        lead = jnp.sum(jnp.where(lane < LEAD, similar[:, :128], 0.0), axis=1, keepdims=True) * (1.0 / LEAD)
        similar = similar - lead * r_ref[...]
        high, low = split(similar)
        high_ref[at, :] = high
        low_ref[at, :] = low
        own_ref[...] += jnp.sum(low.astype(F32) * low.astype(F32), axis=0, keepdims=True)
        for b, (i, j) in enumerate(UPPER):
            if i == j:
                left_high, left_low = high[:, 128 * i : 128 * i + 128], low[:, 128 * i : 128 * i + 128]
                part = dot(left_high, high[:, 128 * i :], (0, 0))
                part += dot(left_high, low[:, 128 * i :], (0, 0)) + dot(left_low, high[:, 128 * i :], (0, 0))
                for e in range(4 - i):
                    in_ref[128 * (b + e) : 128 * (b + e) + 128, :] += part[:, 128 * e : 128 * e + 128]
        return carry

    lax.fori_loop(0, tiles, tile, 0)
    row = lax.broadcasted_iota(jnp.int32, (128, 128), 0)
    col = lax.broadcasted_iota(jnp.int32, (128, 128), 1)
    for b, (i, j) in enumerate(UPPER):
        if i == j:
            in_ref[128 * b : 128 * b + 128, :] += jnp.where(row == col, own_ref[:, 128 * i : 128 * i + 128], 0.0)

    work = cholesky_steps(w_ref, diag_ref)
    mine = core * 640
    theirs = (1 - core) * 640
    axes = ((along_x, NX, x), (along_y, NY, y))
    state = [
        push(in_ref.at[pl.ds(theirs + start, size)], core_in.at[pl.ds(start, size)], other) for start, size in STREAMS
    ]
    stores = [
        pltpu.make_async_copy(high_ref, high_hbm, load.at[tiles + 1]),
        pltpu.make_async_copy(low_ref, low_hbm, load.at[tiles + 2]),
    ]
    for copy in stores:
        copy.start()
    big = []
    for s, (start, size) in enumerate(STREAMS):
        peers, n, pos = axes[s]
        state[s].wait_recv()
        half_sum[pl.ds(start, size), :] = in_ref[pl.ds(mine + start, size), :] + core_in[pl.ds(start, size), :]
        part = size // 4
        copies = []
        for o in range(1, n):
            to = lax.rem(pos + o, n)
            piece = half_sum.at[pl.ds(start + to * part, part)]
            copies.append(push(piece, big_in.at[o - 1, pl.ds(start // 4, part)], peers[o - 1]))
        big.append(copies)
    next(work)
    next(work)
    small = []
    for s, (start, size) in enumerate(STREAMS):
        _, n, pos = axes[s]
        peers, n2, pos2 = axes[1 - s]
        part = size // 4
        arrive(big[s])
        total = half_sum[pl.ds(start + pos * part, part), :]
        for o in range(n - 1):
            total = total + big_in[o, start // 4 : start // 4 + part, :]
        big_sum[start // 4 : start // 4 + part, :] = total
        tiny = part // 4
        copies = []
        for o in range(1, n2):
            to = lax.rem(pos2 + o, n2)
            piece = big_sum.at[pl.ds(start // 4 + to * tiny, tiny)]
            copies.append(push(piece, small_in.at[o - 1, pl.ds(start // 16, tiny)], peers[o - 1]))
        small.append(copies)
    next(work)
    last = []
    for s, (start, size) in enumerate(STREAMS):
        _, n2, pos2 = axes[1 - s]
        tiny = size // 16
        arrive(small[s])
        total = big_sum[pl.ds(start // 4 + pos2 * tiny, tiny), :]
        for o in range(n2 - 1):
            total = total + small_in[o, start // 16 : start // 16 + tiny, :]
        small_sum[start // 16 : start // 16 + tiny, :] = total
        piece = small_sum.at[pl.ds(start // 16, tiny)]
        last.append([push(piece, z_in.at[z, pl.ds(start // 16, tiny)], peer) for peer in along_z])
        z_in[z, start // 16 : start // 16 + tiny, :] = total
    next(work)
    next(work)
    back = []
    for s, (start, size) in enumerate(STREAMS):
        _, n, pos = axes[s]
        peers, n2, pos2 = axes[1 - s]
        part, tiny = size // 4, size // 16
        arrive(last[s])
        total = z_in[0, start // 16 : start // 16 + tiny, :]
        for o in range(1, NZ):
            total = total + z_in[o, start // 16 : start // 16 + tiny, :]
        at = mine + start + pos * part + pos2 * tiny
        out_ref[pl.ds(at, tiny), :] = total
        piece = out_ref.at[pl.ds(at, tiny)]
        back.append([push(piece, piece, peer) for peer in peers])
    next(work)
    far = []
    for s, (start, size) in enumerate(STREAMS):
        peers, n, pos = axes[s]
        part = size // 4
        arrive(back[s])
        piece = out_ref.at[pl.ds(mine + start + pos * part, part)]
        far.append([push(piece, piece, peer) for peer in peers])
    for _ in work:
        pass
    final = []
    for s, (start, size) in enumerate(STREAMS):
        arrive(far[s])
        piece = out_ref.at[pl.ds(mine + start, size)]
        final.append(push(piece, piece, other))
    inverse = lower_blocks(w_ref[...])
    weight = jnp.sum(inverse * r_ref[...], axis=1, keepdims=True) * (1.0 / LEAD)
    tail_ref[...] = inverse + jnp.where(lax.broadcasted_iota(jnp.int32, (512, 512), 1) < LEAD, weight, 0.0)
    arrive(final)
    for copy in stores:
        copy.wait()
    for copy in everything:
        copy.wait_send()


def gram_call(mine, targets, embeddings):
    rows = embeddings.shape[0]
    copies = 2 + 2 * (7 + 3 + 3 + 1) + 2 * (1 + 3 + 3 + 7 + 3 + 3 + 1)
    vmem = pl.BlockSpec(memory_space=pltpu.VMEM)
    return pl.pallas_call(
        gram_kernel,
        out_shape=(
            jax.ShapeDtypeStruct((rows, 512), BF16),
            jax.ShapeDtypeStruct((rows, 512), BF16),
            jax.ShapeDtypeStruct((1280, 128), F32),
            jax.ShapeDtypeStruct((512, 512), F32),
        ),
        in_specs=[pl.BlockSpec(memory_space=pltpu.HBM)] * 3,
        out_specs=(pl.BlockSpec(memory_space=pltpu.HBM),) * 2 + (vmem,) * 2,
        scratch_shapes=[
            pltpu.VMEM((rows, 512), BF16),
            pltpu.VMEM((rows, 512), BF16),
            pltpu.VMEM((2, 256), jnp.int32),
            pltpu.VMEM((rows, 1024), BF16),
            pltpu.VMEM((rows, 1), F32),
            pltpu.VMEM((2, 256, 8, 128), BF16),
            pltpu.VMEM((2048, 128), F32),
            pltpu.VMEM((512, 1024), BF16),
            pltpu.VMEM((1, 512), F32),
            pltpu.VMEM((1, 512), F32),
            pltpu.VMEM((1, 512), F32),
            pltpu.VMEM((1280, 128), F32),
            pltpu.VMEM((512, 512), F32),
            pltpu.VMEM((8, NB, 128), F32),
            pltpu.VMEM((640, 128), F32),
            pltpu.VMEM((3, 160, 128), F32),
            pltpu.VMEM((3, 40, 128), F32),
            pltpu.VMEM((NZ, 40, 128), F32),
            pltpu.VMEM((640, 128), F32),
            pltpu.VMEM((160, 128), F32),
            pltpu.VMEM((40, 128), F32),
            pltpu.SemaphoreType.DMA((rows // TILE + 3,)),
            pltpu.SemaphoreType.DMA((copies,)),
            pltpu.SemaphoreType.DMA((copies,)),
        ],
        compiler_params=pltpu.CompilerParams(collective_id=0, has_side_effects=True, vmem_limit_bytes=52 << 20),
        name="gram",
    )(mine, targets, embeddings)


def basis_kernel(total_rows, gram_ref, tail_ref, high_ref, low_ref, basis_ref, triangle_ref, w_ref, diag_ref, inv_high, inv_low):
    @pl.when(pl.program_id(0) == 0)
    def _():
        for b, (i, j) in enumerate(UPPER):
            w_ref[128 * i : 128 * i + 128, 128 * j : 128 * j + 128] = gram_ref[b] / total_rows
        cholesky_inverse(w_ref, diag_ref)
        w = w_ref[...]
        inv_high[...], inv_low[...] = split(lower_blocks(w))
        row = lax.broadcasted_iota(jnp.int32, (512, 512), 0)
        col = lax.broadcasted_iota(jnp.int32, (512, 512), 1)
        w_ref[...] = jnp.where(row < col, w, 0.0)
        lane = lax.broadcasted_iota(jnp.int32, (NB, 128), 1)
        sub = lax.broadcasted_iota(jnp.int32, (NB, 128), 0)
        for k in range(8):
            left = 128 * (k // 2)
            both = diag_ref[k]
            keep = w_ref[NB * k : NB * k + NB, left : left + 128]
            if k % 2:
                mine = pltpu.roll(both, 64, 1)
                keep = jnp.where(lane >= 64, jnp.where(lane - 64 >= sub, mine, 0.0), keep)
            else:
                keep = jnp.where(lane < 64, jnp.where(lane >= sub, both, 0.0), keep)
            w_ref[NB * k : NB * k + NB, left : left + 128] = keep
        triangle_ref[...] = dot(w_ref[...], tail_ref[...], (1, 1), HI)

    high, low = high_ref[...], low_ref[...]
    for start, depth in ((0, 256), (256, 512)):
        right_high, right_low = inv_high[start : start + 256, :depth], inv_low[start : start + 256, :depth]
        out = dot(low[:, :depth], right_high, (1, 1)) + dot(high[:, :depth], right_low, (1, 1))
        basis_ref[:, start : start + 256] = out + dot(high[:, :depth], right_high, (1, 1))


def basis_call(gram, tail, high, low, total_rows):
    count = high.shape[0] // TILE
    whole = lambda shape: pl.BlockSpec(shape, lambda i: (0,) * len(shape))
    tile = pl.BlockSpec((TILE, 512), lambda i: (i, 0))
    return pl.pallas_call(
        functools.partial(basis_kernel, total_rows),
        grid=(count,),
        out_shape=(jax.ShapeDtypeStruct(high.shape, F32), jax.ShapeDtypeStruct((512, 512), F32)),
        in_specs=[whole((10, 128, 128)), whole((512, 512)), tile, tile],
        out_specs=(tile, whole((512, 512))),
        scratch_shapes=[
            pltpu.VMEM((512, 512), F32),
            pltpu.VMEM((8, NB, 128), F32),
            pltpu.VMEM((512, 512), BF16),
            pltpu.VMEM((512, 512), BF16),
        ],
        compiler_params=pltpu.CompilerParams(vmem_limit_bytes=52 << 20, dimension_semantics=("arbitrary",)),
        name="basis",
    )(gram, tail, high, low)


def pick_kernel(row_count, pivots_ref, emb_ref, mine_ref, targets_ref, block_ref, sems):
    start = (lax.axis_index("bank") * 2 + lax.axis_index("sub")) * row_count
    pivots = pivots_ref[...]
    inside = (pivots >= start) & (pivots < start + row_count)
    copies, offsets = [], []
    for s in range(2):
        local = jnp.sum(jnp.where(inside[s : s + 1], pivots[s : s + 1] - start, 0))
        first = pl.multiple_of((local // 16) * 16, 16)
        copy = pltpu.make_async_copy(emb_ref.at[pl.ds(first, 16)], block_ref.at[s], sems.at[s])
        copy.start()
        copies.append(copy)
        offsets.append(local - first)
    owner = jnp.floor((pivots.astype(F32) + 0.5) * (1.0 / row_count)).astype(jnp.int32)
    bank, core = owner >> 1, owner & 1
    bx, bz, by = bank & (NX - 1), (bank >> 2) & (NZ - 1), bank >> 5
    first = core * 128 + (by * NX + bx) * NZ + bz
    second = core * 128 + (bx * NY + by) * NZ + bz
    targets_ref[...] = jnp.where(lax.broadcasted_iota(jnp.int32, (2, 256), 0) == 0, first, second)
    for s in range(2):
        copies[s].wait()
        rows = block_ref[s].astype(F32)
        keep = lax.broadcasted_iota(jnp.int32, (16, 1024), 0) == offsets[s]
        row = jnp.sum(jnp.where(keep, rows, 0.0), axis=0, keepdims=True)
        mine_ref[s] = jnp.concatenate([row[:, 128 * q : 128 * q + 128] for q in range(8)], axis=0).astype(BF16)


def pick_rows(pivots, embeddings):
    return pl.pallas_call(
        functools.partial(pick_kernel, embeddings.shape[0]),
        out_shape=(jax.ShapeDtypeStruct((2, 8, 128), BF16), jax.ShapeDtypeStruct((2, 256), jnp.int32)),
        in_specs=[pl.BlockSpec(memory_space=pltpu.VMEM), pl.BlockSpec(memory_space=pl.ANY)],
        out_specs=(pl.BlockSpec(memory_space=pltpu.VMEM),) * 2,
        scratch_shapes=[pltpu.VMEM((2, 16, 1024), BF16), pltpu.SemaphoreType.DMA((2,))],
        compiler_params=pltpu.CompilerParams(vmem_limit_bytes=52 << 20),
        name="pick_rows",
    )(pivots, embeddings)


def per_device(embeddings, pivots):
    total_rows = embeddings.shape[0] * lax.axis_size(("bank", "sub"))
    mine, targets = pick_rows(pivots, embeddings)
    high, low, gram, tail = gram_call(mine, targets, embeddings)
    gram = gram.reshape(10, 128, 128)
    return basis_call(gram, tail, high, low, float(total_rows))


def solution(mesh):
    in_specs = (P(("bank", "sub"), None), P())
    out_specs = (P(("bank", "sub"), None), P())
    return jax.shard_map(per_device, mesh=mesh, in_specs=in_specs, out_specs=out_specs, check_vma=False)
```

```python
import functools

import jax
import jax.numpy as jnp
from jax import lax
from jax.experimental import pallas as pl
from jax.experimental.pallas import tpu as pltpu
from jax.sharding import PartitionSpec as P

HI = lax.Precision.HIGHEST
F32 = jnp.float32
BF16 = jnp.bfloat16
P_SIZE = 256
NX, NY, NZ = 4, 4, 8
NB = 64
TILE = 512
UPPER = [(i, j) for i in range(4) for j in range(i, 4)]
MESH = pl.DeviceIdType.MESH


def dot(a, b, dims, precision=None):
    return lax.dot_general(a, b, ((dims[:1], dims[1:]), ((), ())), precision=precision, preferred_element_type=F32)


def base_block(rows):
    count = NB // 8
    rows = list(rows)
    sub = lax.broadcasted_iota(jnp.int32, (8, 128), 0)
    lane = lax.broadcasted_iota(jnp.int32, (8, 128), 1)
    full = lambda v: jnp.broadcast_to(v, (8, 128))

    def fetch(k):
        spread = lambda v, j: full(jnp.sum(jnp.where(lane == j, v, 0.0), axis=1, keepdims=True))
        return {t: [spread(rows[t], 8 * k + c) for c in range(8)] for t in range(k, count)}

    out = []
    now = fetch(0)
    for k in range(count):
        later = fetch(k + 1) if k + 1 < count else None
        scale = jnp.zeros((8, 128), F32)
        for c in range(8):
            pivot = full(now[k][c][c : c + 1, :])
            pivot_row = full(rows[k][c : c + 1, :])
            ahead = [full(now[k][e][c : c + 1, :]) for e in range(c + 1, 8)]
            if later is not None:
                beyond = [full(now[k + 1][c][e : e + 1, :]) for e in range(8)]
            inverse = 1.0 / pivot
            scale = jnp.where(sub == c, pivot, scale)
            for t in range(k, count):
                column = jnp.where(sub > c, now[t][c], 0.0) if t == k else now[t][c]
                mult = column * inverse
                rows[t] = rows[t] - mult * pivot_row
                for e in range(c + 1, 8):
                    now[t][e] = now[t][e] - mult * ahead[e - c - 1]
                if t > k:
                    for e in range(8):
                        later[t][e] = later[t][e] - mult * beyond[e]
        out.append(rows[k] * lax.rsqrt(scale))
        now = later
    return out


def cholesky_steps(w_ref, diag_ref):
    n = w_ref.shape[0]
    lane = lax.broadcasted_iota(jnp.int32, (8, 128), 1)
    sub = lax.broadcasted_iota(jnp.int32, (8, 128), 0)
    block = w_ref[0:NB, 0:128]
    for k in range(n // NB):
        r0, r1 = k * NB, k * NB + NB
        rows = []
        for t in range(NB // 8):
            eye = jnp.where(lane - NB == sub + 8 * t, 1.0, 0.0)
            rows.append(jnp.where(lane < NB, block[8 * t : 8 * t + 8, :], eye))
        both = jnp.concatenate(base_block(rows), axis=0)
        diag_ref[k] = both
        inverse = both[:, NB:]
        if r1 < n:
            left = (r1 // 128) * 128
            ahead, block = w_ref[r0:r1, left : left + 128], w_ref[r1 : r1 + NB, left : left + 128]
            if r1 % 128:
                ahead, block = pltpu.roll(ahead, NB, 1), pltpu.roll(block, NB, 1)
            ahead = dot(inverse, ahead, (1, 0), HI)
            block = block - dot(ahead[:, :NB], ahead, (0, 0), HI)
        yield
        wide = w_ref[r0:r1, :]
        col = lax.broadcasted_iota(jnp.int32, (NB, n), 1)
        row = lax.broadcasted_iota(jnp.int32, (NB, n), 0)
        wide = jnp.where((col >= r0) & (col < r1), jnp.where(col - r0 == row, 1.0, 0.0), wide)
        strip = dot(inverse, wide, (1, 0), HI)
        w_ref[r0:r1, :] = strip
        if r1 < n:
            update = dot(strip[:, r1:], strip, (0, 0), HI)
            current = w_ref[r1:, :]
            col = lax.broadcasted_iota(jnp.int32, (n - r1, n), 1)
            w_ref[r1:, :] = jnp.where((col >= r0) & (col < r1), 0.0, current) - update


def cholesky_inverse(w_ref, diag_ref):
    for _ in cholesky_steps(w_ref, diag_ref):
        pass


def lower_blocks(w):
    n = w.shape[0]
    row = lax.broadcasted_iota(jnp.int32, (n, n), 0)
    col = lax.broadcasted_iota(jnp.int32, (n, n), 1)
    return jnp.where(row >= col, w, 0.0)


def coords():
    bank = lax.axis_index("bank")
    core = lax.axis_index("sub")
    x = lax.rem(bank, NX)
    z = lax.rem(bank // NX, NZ)
    y = bank // (NX * NZ)
    return x, y, z, core


def bank_of(x, y, z):
    return (y * NZ + z) * NX + x


def axis_peers(x, y, z, core):
    along_x = [(bank_of(lax.rem(x + o, NX), y, z), core) for o in range(1, NX)]
    along_y = [(bank_of(x, lax.rem(y + o, NY), z), core) for o in range(1, NY)]
    along_z = [(bank_of(x, y, lax.rem(z + o, NZ)), core) for o in range(1, NZ)]
    return along_x, along_y, along_z


LEAD = 16
STREAMS = ((0, 384), (384, 256))


def split(v):
    high = v.astype(BF16)
    return high, (v - high.astype(F32)).astype(BF16)


def gram_kernel(
    mine_hbm, targets_hbm, emb_hbm, high_hbm, low_hbm, out_ref, tail_ref,
    high_ref, low_ref, targets_ref, emb_ref, norms_ref, rows_ref, wide_ref, chosen_ref, norm_ref, r_ref, own_ref, in_ref, w_ref, diag_ref,
    core_in, big_in, small_in, z_in, half_sum, big_sum, small_sum, load, send, recv,
):
    x, y, z, core = coords()
    other = (lax.axis_index("bank"), 1 - core)
    along_x, along_y, along_z = axis_peers(x, y, z, core)
    row_count = emb_hbm.shape[0]
    tiles = row_count // TILE
    everything = []
    count = [2]

    def push(src, dst, peer):
        i = count[0]
        count[0] += 1
        copy = pltpu.make_async_remote_copy(
            src_ref=src, dst_ref=dst, send_sem=send.at[i], recv_sem=recv.at[i], device_id=peer, device_id_type=MESH
        )
        copy.start()
        everything.append(copy)
        return copy

    def arrive(copies):
        for copy in copies:
            copy.wait_recv()

    half = NX * NY * NZ
    base = core * half
    slot_a = base + (y * NX + x) * NZ + z
    slot_b = base + (x * NY + y) * NZ + z
    loads = [
        pltpu.make_async_copy(emb_hbm.at[pl.ds(t * TILE, TILE)], emb_ref.at[pl.ds(t * TILE, TILE)], load.at[t])
        for t in range(tiles)
    ]
    local = [
        pltpu.make_async_copy(mine_hbm.at[0], rows_ref.at[0, slot_a], send.at[0]),
        pltpu.make_async_copy(mine_hbm.at[1], rows_ref.at[1, slot_b], send.at[1]),
        pltpu.make_async_copy(targets_hbm, targets_ref, load.at[tiles]),
    ]
    for copy in local + loads:
        copy.start()
    peers = [other] + along_x + along_y + along_z
    barrier = pltpu.get_barrier_semaphore()
    for peer in peers:
        pl.semaphore_signal(barrier, inc=1, device_id=peer, device_id_type=MESH)

    def norms(first, last):
        for t in range(first, last):
            loads[t].wait()

        def body(i, carry):
            at = pl.ds(pl.multiple_of(i * 64, 64), 64)
            wide = emb_ref[at, :].astype(F32)
            norms_ref[at, :] = jnp.sum(wide * wide, axis=1, keepdims=True)
            return carry

        lax.fori_loop(first * (TILE // 64), last * (TILE // 64), body, 0)

    def share(step, start, size, to):
        part = rows_ref.at[step, pl.ds(start, size)]
        return [push(part, part, peer) for peer in to]

    for copy in local:
        copy.wait()
    pl.semaphore_wait(barrier, len(peers))
    first_a = share(0, slot_a, 1, along_z)
    first_b = share(1, slot_b, 1, along_z)
    norms(0, 2)
    arrive(first_a)
    second_a = share(0, slot_a - z, NZ, along_x)
    arrive(first_b)
    second_b = share(1, slot_b - z, NZ, along_y)
    norms(2, 4)
    arrive(second_a)
    third_a = share(0, base + y * NX * NZ, NX * NZ, along_y)
    arrive(second_b)
    third_b = share(1, base + x * NY * NZ, NY * NZ, along_x)
    norms(4, tiles)
    arrive(third_a)
    last_a = share(0, base, half, [other])
    arrive(third_b)
    last_b = share(1, base, half, [other])

    for s, copies in ((0, last_a), (1, last_b)):
        slot = lax.broadcasted_iota(jnp.int32, (256, 256), 0)
        pick = jnp.where(slot == targets_ref[s : s + 1, :], 1.0, 0.0).astype(BF16)
        arrive(copies)
        wide_ref[...] = rows_ref[s].reshape(2048, 128).astype(F32)
        for q in range(8):
            part = wide_ref[pl.ds(q, 256, stride=8), :].astype(BF16)
            chosen_ref[256 * s : 256 * s + 256, 128 * q : 128 * q + 128] = dot(pick, part, (0, 0)).astype(BF16)
    dots = dot(chosen_ref[...], chosen_ref[...], (1, 1))
    row = lax.broadcasted_iota(jnp.int32, (512, 512), 0)
    col = lax.broadcasted_iota(jnp.int32, (512, 512), 1)
    own = jnp.where(row == col, dots, 0.0)
    norm_row = jnp.sum(own, axis=0, keepdims=True)
    norm_ref[...] = norm_row
    block = dots / (jnp.sum(own, axis=1, keepdims=True) + norm_row - dots)
    w_ref[...] = block
    lead = jnp.sum(jnp.where(col < LEAD, block, 0.0), axis=1, keepdims=True) * (1.0 / LEAD)
    use = (row >= LEAD) & (row != col)
    above = jnp.sum(jnp.where(use, block * lead, 0.0), axis=0, keepdims=True)
    below = jnp.sum(jnp.where(use, lead * lead, 0.0), axis=0, keepdims=True)
    ratio = above / jnp.where(below > 0.0, below, 1.0)
    ratio = jnp.where(below > 0.0, jnp.clip(ratio, -4.0, 4.0), 0.0)
    r_ref[...] = jnp.where(lax.broadcasted_iota(jnp.int32, (1, 512), 1) < LEAD, 0.0, ratio)
    in_ref[...] = jnp.zeros_like(in_ref)
    own_ref[...] = jnp.zeros_like(own_ref)

    def tile(t, carry):
        at = pl.ds(pl.multiple_of(t * TILE, TILE), TILE)
        dots = dot(emb_ref[at, :], chosen_ref[...], (1, 1))
        similar = dots / (norms_ref[at, :] + norm_ref[...] - dots)
        lane = lax.broadcasted_iota(jnp.int32, (TILE, 128), 1)
        lead = jnp.sum(jnp.where(lane < LEAD, similar[:, :128], 0.0), axis=1, keepdims=True) * (1.0 / LEAD)
        similar = similar - lead * r_ref[...]
        high, low = split(similar)
        high_ref[at, :] = high
        low_ref[at, :] = low
        own_ref[...] += jnp.sum(low.astype(F32) * low.astype(F32), axis=0, keepdims=True)
        for b, (i, j) in enumerate(UPPER):
            if i == j:
                left_high, left_low = high[:, 128 * i : 128 * i + 128], low[:, 128 * i : 128 * i + 128]
                part = dot(left_high, high[:, 128 * i :], (0, 0))
                part += dot(left_high, low[:, 128 * i :], (0, 0)) + dot(left_low, high[:, 128 * i :], (0, 0))
                for e in range(4 - i):
                    in_ref[128 * (b + e) : 128 * (b + e) + 128, :] += part[:, 128 * e : 128 * e + 128]
        return carry

    lax.fori_loop(0, tiles, tile, 0)
    row = lax.broadcasted_iota(jnp.int32, (128, 128), 0)
    col = lax.broadcasted_iota(jnp.int32, (128, 128), 1)
    for b, (i, j) in enumerate(UPPER):
        if i == j:
            in_ref[128 * b : 128 * b + 128, :] += jnp.where(row == col, own_ref[:, 128 * i : 128 * i + 128], 0.0)

    work = cholesky_steps(w_ref, diag_ref)
    mine = core * 640
    theirs = (1 - core) * 640
    axes = ((along_x, NX, x), (along_y, NY, y))
    state = [
        push(in_ref.at[pl.ds(theirs + start, size)], core_in.at[pl.ds(start, size)], other) for start, size in STREAMS
    ]
    stores = [
        pltpu.make_async_copy(high_ref, high_hbm, load.at[tiles + 1]),
        pltpu.make_async_copy(low_ref, low_hbm, load.at[tiles + 2]),
    ]
    for copy in stores:
        copy.start()
    big = []
    for s, (start, size) in enumerate(STREAMS):
        peers, n, pos = axes[s]
        state[s].wait_recv()
        half_sum[pl.ds(start, size), :] = in_ref[pl.ds(mine + start, size), :] + core_in[pl.ds(start, size), :]
        part = size // 4
        copies = []
        for o in range(1, n):
            to = lax.rem(pos + o, n)
            piece = half_sum.at[pl.ds(start + to * part, part)]
            copies.append(push(piece, big_in.at[o - 1, pl.ds(start // 4, part)], peers[o - 1]))
        big.append(copies)
    next(work)
    next(work)
    small = []
    for s, (start, size) in enumerate(STREAMS):
        _, n, pos = axes[s]
        peers, n2, pos2 = axes[1 - s]
        part = size // 4
        arrive(big[s])
        total = half_sum[pl.ds(start + pos * part, part), :]
        for o in range(n - 1):
            total = total + big_in[o, start // 4 : start // 4 + part, :]
        big_sum[start // 4 : start // 4 + part, :] = total
        tiny = part // 4
        copies = []
        for o in range(1, n2):
            to = lax.rem(pos2 + o, n2)
            piece = big_sum.at[pl.ds(start // 4 + to * tiny, tiny)]
            copies.append(push(piece, small_in.at[o - 1, pl.ds(start // 16, tiny)], peers[o - 1]))
        small.append(copies)
    next(work)
    last = []
    for s, (start, size) in enumerate(STREAMS):
        _, n2, pos2 = axes[1 - s]
        tiny = size // 16
        arrive(small[s])
        total = big_sum[pl.ds(start // 4 + pos2 * tiny, tiny), :]
        for o in range(n2 - 1):
            total = total + small_in[o, start // 16 : start // 16 + tiny, :]
        small_sum[start // 16 : start // 16 + tiny, :] = total
        piece = small_sum.at[pl.ds(start // 16, tiny)]
        last.append([push(piece, z_in.at[z, pl.ds(start // 16, tiny)], peer) for peer in along_z])
        z_in[z, start // 16 : start // 16 + tiny, :] = total
    next(work)
    next(work)
    back = []
    for s, (start, size) in enumerate(STREAMS):
        _, n, pos = axes[s]
        peers, n2, pos2 = axes[1 - s]
        part, tiny = size // 4, size // 16
        arrive(last[s])
        total = z_in[0, start // 16 : start // 16 + tiny, :]
        for o in range(1, NZ):
            total = total + z_in[o, start // 16 : start // 16 + tiny, :]
        at = mine + start + pos * part + pos2 * tiny
        out_ref[pl.ds(at, tiny), :] = total
        piece = out_ref.at[pl.ds(at, tiny)]
        back.append([push(piece, piece, peer) for peer in peers])
    next(work)
    far = []
    for s, (start, size) in enumerate(STREAMS):
        peers, n, pos = axes[s]
        part = size // 4
        arrive(back[s])
        piece = out_ref.at[pl.ds(mine + start + pos * part, part)]
        far.append([push(piece, piece, peer) for peer in peers])
    for _ in work:
        pass
    final = []
    for s, (start, size) in enumerate(STREAMS):
        arrive(far[s])
        piece = out_ref.at[pl.ds(mine + start, size)]
        final.append(push(piece, piece, other))
    inverse = lower_blocks(w_ref[...])
    weight = jnp.sum(inverse * r_ref[...], axis=1, keepdims=True) * (1.0 / LEAD)
    tail_ref[...] = inverse + jnp.where(lax.broadcasted_iota(jnp.int32, (512, 512), 1) < LEAD, weight, 0.0)
    arrive(final)
    for copy in stores:
        copy.wait()
    for copy in everything:
        copy.wait_send()


def gram_call(mine, targets, embeddings):
    rows = embeddings.shape[0]
    copies = 2 + 2 * (7 + 3 + 3 + 1) + 2 * (1 + 3 + 3 + 7 + 3 + 3 + 1)
    vmem = pl.BlockSpec(memory_space=pltpu.VMEM)
    return pl.pallas_call(
        gram_kernel,
        out_shape=(
            jax.ShapeDtypeStruct((rows, 512), BF16),
            jax.ShapeDtypeStruct((rows, 512), BF16),
            jax.ShapeDtypeStruct((1280, 128), F32),
            jax.ShapeDtypeStruct((512, 512), F32),
        ),
        in_specs=[pl.BlockSpec(memory_space=pltpu.HBM)] * 3,
        out_specs=(pl.BlockSpec(memory_space=pltpu.HBM),) * 2 + (vmem,) * 2,
        scratch_shapes=[
            pltpu.VMEM((rows, 512), BF16),
            pltpu.VMEM((rows, 512), BF16),
            pltpu.VMEM((2, 256), jnp.int32),
            pltpu.VMEM((rows, 1024), BF16),
            pltpu.VMEM((rows, 1), F32),
            pltpu.VMEM((2, 256, 8, 128), BF16),
            pltpu.VMEM((2048, 128), F32),
            pltpu.VMEM((512, 1024), BF16),
            pltpu.VMEM((1, 512), F32),
            pltpu.VMEM((1, 512), F32),
            pltpu.VMEM((1, 512), F32),
            pltpu.VMEM((1280, 128), F32),
            pltpu.VMEM((512, 512), F32),
            pltpu.VMEM((8, NB, 128), F32),
            pltpu.VMEM((640, 128), F32),
            pltpu.VMEM((3, 160, 128), F32),
            pltpu.VMEM((3, 40, 128), F32),
            pltpu.VMEM((NZ, 40, 128), F32),
            pltpu.VMEM((640, 128), F32),
            pltpu.VMEM((160, 128), F32),
            pltpu.VMEM((40, 128), F32),
            pltpu.SemaphoreType.DMA((rows // TILE + 3,)),
            pltpu.SemaphoreType.DMA((copies,)),
            pltpu.SemaphoreType.DMA((copies,)),
        ],
        compiler_params=pltpu.CompilerParams(collective_id=0, has_side_effects=True, vmem_limit_bytes=52 << 20),
        name="gram",
    )(mine, targets, embeddings)


def basis_kernel(total_rows, gram_ref, tail_ref, high_ref, low_ref, basis_ref, triangle_ref, w_ref, diag_ref, inv_high, inv_low):
    @pl.when(pl.program_id(0) == 0)
    def _():
        for b, (i, j) in enumerate(UPPER):
            w_ref[128 * i : 128 * i + 128, 128 * j : 128 * j + 128] = gram_ref[b] / total_rows
        cholesky_inverse(w_ref, diag_ref)
        w = w_ref[...]
        inv_high[...], inv_low[...] = split(lower_blocks(w))
        row = lax.broadcasted_iota(jnp.int32, (512, 512), 0)
        col = lax.broadcasted_iota(jnp.int32, (512, 512), 1)
        w_ref[...] = jnp.where(row < col, w, 0.0)
        lane = lax.broadcasted_iota(jnp.int32, (NB, 128), 1)
        sub = lax.broadcasted_iota(jnp.int32, (NB, 128), 0)
        for k in range(8):
            left = 128 * (k // 2)
            both = diag_ref[k]
            keep = w_ref[NB * k : NB * k + NB, left : left + 128]
            if k % 2:
                mine = pltpu.roll(both, 64, 1)
                keep = jnp.where(lane >= 64, jnp.where(lane - 64 >= sub, mine, 0.0), keep)
            else:
                keep = jnp.where(lane < 64, jnp.where(lane >= sub, both, 0.0), keep)
            w_ref[NB * k : NB * k + NB, left : left + 128] = keep
        triangle_ref[:256, :256] = dot(w_ref[:256, :256], tail_ref[:256, :256], (1, 1), HI)
        triangle_ref[:256, 256:] = dot(w_ref[:256, :], tail_ref[256:, :], (1, 1), HI)
        triangle_ref[256:, 256:] = dot(w_ref[256:, 256:], tail_ref[256:, 256:], (1, 1), HI)
        triangle_ref[256:, :256] = jnp.zeros((256, 256), F32)

    high, low = high_ref[...], low_ref[...]
    for start, depth in ((0, 256), (256, 512)):
        right_high, right_low = inv_high[start : start + 256, :depth], inv_low[start : start + 256, :depth]
        out = dot(low[:, :depth], right_high, (1, 1)) + dot(high[:, :depth], right_low, (1, 1))
        basis_ref[:, start : start + 256] = out + dot(high[:, :depth], right_high, (1, 1))


def basis_call(gram, tail, high, low, total_rows):
    count = high.shape[0] // TILE
    whole = lambda shape: pl.BlockSpec(shape, lambda i: (0,) * len(shape))
    tile = pl.BlockSpec((TILE, 512), lambda i: (i, 0))
    return pl.pallas_call(
        functools.partial(basis_kernel, total_rows),
        grid=(count,),
        out_shape=(jax.ShapeDtypeStruct(high.shape, F32), jax.ShapeDtypeStruct((512, 512), F32)),
        in_specs=[whole((10, 128, 128)), whole((512, 512)), tile, tile],
        out_specs=(tile, whole((512, 512))),
        scratch_shapes=[
            pltpu.VMEM((512, 512), F32),
            pltpu.VMEM((8, NB, 128), F32),
            pltpu.VMEM((512, 512), BF16),
            pltpu.VMEM((512, 512), BF16),
        ],
        compiler_params=pltpu.CompilerParams(vmem_limit_bytes=52 << 20, dimension_semantics=("arbitrary",)),
        name="basis",
    )(gram, tail, high, low)


def pick_kernel(row_count, pivots_ref, emb_ref, mine_ref, targets_ref, block_ref, sems):
    start = (lax.axis_index("bank") * 2 + lax.axis_index("sub")) * row_count
    pivots = pivots_ref[...]
    inside = (pivots >= start) & (pivots < start + row_count)
    copies, offsets = [], []
    for s in range(2):
        local = jnp.sum(jnp.where(inside[s : s + 1], pivots[s : s + 1] - start, 0))
        first = pl.multiple_of((local // 16) * 16, 16)
        copy = pltpu.make_async_copy(emb_ref.at[pl.ds(first, 16)], block_ref.at[s], sems.at[s])
        copy.start()
        copies.append(copy)
        offsets.append(local - first)
    owner = jnp.floor((pivots.astype(F32) + 0.5) * (1.0 / row_count)).astype(jnp.int32)
    bank, core = owner >> 1, owner & 1
    bx, bz, by = bank & (NX - 1), (bank >> 2) & (NZ - 1), bank >> 5
    first = core * 128 + (by * NX + bx) * NZ + bz
    second = core * 128 + (bx * NY + by) * NZ + bz
    targets_ref[...] = jnp.where(lax.broadcasted_iota(jnp.int32, (2, 256), 0) == 0, first, second)
    for s in range(2):
        copies[s].wait()
        rows = block_ref[s].astype(F32)
        keep = lax.broadcasted_iota(jnp.int32, (16, 1024), 0) == offsets[s]
        row = jnp.sum(jnp.where(keep, rows, 0.0), axis=0, keepdims=True)
        mine_ref[s] = jnp.concatenate([row[:, 128 * q : 128 * q + 128] for q in range(8)], axis=0).astype(BF16)


def pick_rows(pivots, embeddings):
    return pl.pallas_call(
        functools.partial(pick_kernel, embeddings.shape[0]),
        out_shape=(jax.ShapeDtypeStruct((2, 8, 128), BF16), jax.ShapeDtypeStruct((2, 256), jnp.int32)),
        in_specs=[pl.BlockSpec(memory_space=pltpu.VMEM), pl.BlockSpec(memory_space=pl.ANY)],
        out_specs=(pl.BlockSpec(memory_space=pltpu.VMEM),) * 2,
        scratch_shapes=[pltpu.VMEM((2, 16, 1024), BF16), pltpu.SemaphoreType.DMA((2,))],
        compiler_params=pltpu.CompilerParams(vmem_limit_bytes=52 << 20),
        name="pick_rows",
    )(pivots, embeddings)


def per_device(embeddings, pivots):
    total_rows = embeddings.shape[0] * lax.axis_size(("bank", "sub"))
    mine, targets = pick_rows(pivots, embeddings)
    high, low, gram, tail = gram_call(mine, targets, embeddings)
    gram = gram.reshape(10, 128, 128)
    return basis_call(gram, tail, high, low, float(total_rows))


def solution(mesh):
    in_specs = (P(("bank", "sub"), None), P())
    out_specs = (P(("bank", "sub"), None), P())
    return jax.shard_map(per_device, mesh=mesh, in_specs=in_specs, out_specs=out_specs, check_vma=False)
```
